256 devices in a mesh: zg: 8 (over z), zl: 32 (over x, y, core).
Axes of the slice: x: 4, y: 4, z: 8, core: 2. Of those that a mesh axis runs over, the one named last changes fastest.
Arguments:
- brick_data: float32 [16384, 16, 256], P(('zg', 'zl')), may hold values from -6 to 6
- brick_xy: int32 [2, 16384], P(None, ('zg', 'zl')), may hold values from 0 to 31, as said below
- brick_live: int32 [4, 256], P(None, ('zg', 'zl')), may hold values from 1 to 16, as said below
Outputs:
- pressure_real: float32 [512, 257, 512], P(('zg', 'zl'))
- pressure_imag: float32 [512, 257, 512], P(('zg', 'zl'))
The draws below stay inside these ranges and needn't reach their ends.
Inputs may be any that keep to these rules, and one draw needn't show every extreme that they name: brick_live[q, d] counts the live slots of owner d in layer q; the live ones are the first; in every layer some owner has all 16 slots live. `brick_xy`: all slots of one brick layer of one z group (live or not) sit at distinct brick positions.
All inputs are finite; a program needn't handle non-finite values.
Results may differ from the reference program's by a relative error of at most 0.00011.
Values sent between devices are 32-bit elements; how exact they have to be, the bound alone decides.
No kernel may reach another device: no remote copies, remote signals or barrier semaphores. Data moves between devices by JAX's collectives and lax.ppermute only.
A program may use at most 64 MiB of HBM per device.

```python
import math
import jax
import jax.numpy as jnp
from jax import lax

PLANE = 512
BRICK = 16
CAP = 16
KX = 257
LAYERS = 4
NZ = 512
BRICKS = 16384
N_ZG = 8
N_ZL = 32
DEVICES = 256


def draw_brick_live(key, part):
    first = jax.random.randint(jax.random.fold_in(key, 11), (LAYERS, DEVICES), 1, CAP + 1)
    second = jax.random.randint(jax.random.fold_in(key, 12), (LAYERS, DEVICES), 1, CAP + 1)
    counts = jnp.minimum(first, second)
    busiest = jax.random.randint(jax.random.fold_in(key, 13), (LAYERS, 1), 0, DEVICES)
    owners = jnp.arange(DEVICES, dtype=jnp.int32)[None, :]
    return jnp.where(owners == busiest, CAP, counts).astype(jnp.int32)


def draw_brick_xy(key, part):
    groups = DEVICES // N_ZL
    blocks = PLANE // BRICK
    keys = jax.random.split(jax.random.fold_in(key, 21), groups * LAYERS)
    orders = jax.vmap(lambda single: jax.random.permutation(single, blocks * blocks))(keys)
    chosen = orders[:, :N_ZL * CAP].reshape(groups, LAYERS, N_ZL, CAP)
    chosen = jnp.transpose(chosen, (0, 2, 1, 3)).reshape(-1)
    return jnp.stack([chosen % blocks, chosen // blocks]).astype(jnp.int32)


def block_levels(stream_key, extent, shards, smallest, largest):
    loudness, own = 1.0, jax.random.fold_in(stream_key, 6)
    for axis_at, shards_of in shards:
        draws = jnp.exp(jax.random.uniform(jax.random.fold_in(own, axis_at), (shards_of,), jnp.float32, smallest / len(shards), largest / len(shards)))
        loudness = loudness * jnp.repeat(draws, extent[axis_at] // shards_of).reshape([-1 if axis == axis_at else 1 for axis in range(len(extent))])
    return loudness


def gaussian(stream_key, shape, spread, most, shards=(), kind=jnp.bfloat16):
    loudness = block_levels(stream_key, shape, shards, -0.22, 0.18) if shards else 1.0
    values = jax.random.normal(stream_key, shape, jnp.float32) * spread * loudness
    return jnp.minimum(jnp.maximum(values, -most), most).astype(kind)


def setup_inputs(seed: int = 0) -> dict:
    seeds = jax.random.split(jax.random.key(seed), 4)
    brick_data = gaussian(seeds[0], (BRICKS, BRICK, BRICK * BRICK), 1.0, 6.0, ((0, 256),), jnp.float32)
    brick_xy = draw_brick_xy(jax.random.fold_in(seeds[3], 71), 0)
    brick_live = draw_brick_live(jax.random.fold_in(seeds[3], 71), 0)
    return dict(brick_data=brick_data, brick_xy=brick_xy, brick_live=brick_live)


SCREEN = 0.25

def reverse_bits(values, digits):
    result = jnp.zeros_like(values)
    for digit in range(digits):
        result = result | (values >> digit & 1) << digits - 1 - digit
    return result

def group_slab(inputs):
    group_data, group_slots = inputs
    blocks = PLANE // BRICK
    slab = jnp.zeros((LAYERS * blocks * blocks, BRICK, BRICK * BRICK), group_data.dtype)
    slab = slab.at[group_slots].add(group_data)
    slab = slab.reshape(LAYERS, blocks, blocks, BRICK, BRICK, BRICK)
    slab = jnp.transpose(slab, (0, 3, 1, 4, 2, 5)).reshape(LAYERS * BRICK, PLANE, PLANE)
    return jnp.fft.fft(jnp.fft.rfft(slab, axis=2), axis=1)

def reference(brick_data, brick_xy, brick_live):
    owners = N_ZG * N_ZL
    blocks = PLANE // BRICK
    live = jnp.arange(CAP, dtype=jnp.int32)[None, None, :] < jnp.transpose(brick_live)[:, :, None]
    masked = brick_data.reshape(owners, LAYERS, CAP, BRICK, BRICK * BRICK) * live[:, :, :, None, None].astype(brick_data.dtype)
    layer_ids = jnp.arange(LAYERS, dtype=jnp.int32)[None, :, None]
    places = (brick_xy[1] * blocks + brick_xy[0]).reshape(owners, LAYERS, CAP)
    slots = (layer_ids * (blocks * blocks) + places).reshape(N_ZG, -1).astype(jnp.int32)
    group_data = masked.reshape(N_ZG, N_ZL * LAYERS * CAP, BRICK, BRICK * BRICK)
    spectrum = lax.map(group_slab, (group_data, slots))
    spectrum = jnp.fft.fft(spectrum.reshape(NZ, PLANE, KX), axis=0)
    order = reverse_bits(jnp.arange(NZ, dtype=jnp.int32), NZ.bit_length() - 1)
    spectrum = jnp.transpose(spectrum[order], (0, 2, 1))
    along_z = 4.0 * jnp.sin(jnp.pi * order.astype(jnp.float32) / NZ) ** 2
    along_x = 4.0 * jnp.sin(jnp.pi * jnp.arange(KX, dtype=jnp.float32) / PLANE) ** 2
    along_y = 4.0 * jnp.sin(jnp.pi * jnp.arange(PLANE, dtype=jnp.float32) / PLANE) ** 2
    denom = along_z[:, None, None] + along_x[None, :, None] + along_y[None, None, :] + SCREEN
    factor = -(1.0 / math.sqrt(PLANE * PLANE * NZ)) / denom
    pressure_real = (jnp.real(spectrum) * factor).astype(jnp.float32)
    pressure_imag = (jnp.imag(spectrum) * factor).astype(jnp.float32)
    return (pressure_real, pressure_imag)
```

```python
import math

import jax
import jax.numpy as jnp
import numpy as np
from jax import lax
from jax.experimental import pallas as pl
from jax.experimental.pallas import tpu as pltpu
from jax.sharding import PartitionSpec as P

AXES = ("zg", "zl")
NZ = 512
PLANE = 512
BRICK = 16
BLOCKS = 32
LAYERS = 4
CAP = 16
GROUPS = 8
DEVICES = 256
KX = 257
SLOTS = LAYERS * CAP
SITES = BLOCKS * BLOCKS
SCREEN = 0.25
BF16 = jnp.bfloat16
F32 = jnp.float32


def reverse_bits(values, digits):
    result = values * 0
    for digit in range(digits):
        result = result | ((values >> digit) & 1) << (digits - 1 - digit)
    return result


def halves_np(table):
    high = table.astype(np.float32).astype(jnp.bfloat16)
    low = (table - high.astype(np.float64)).astype(np.float32).astype(jnp.bfloat16)
    return high, low


def lattice_tables():
    bx, by = np.divmod(np.arange(SITES), BLOCKS)
    kx, ky = np.divmod(np.arange(SITES), BLOCKS)
    turn = (bx[:, None] * kx[None, :] + by[:, None] * ky[None, :]) % BLOCKS
    angle = 2.0 * np.pi * turn / BLOCKS
    return halves_np(np.concatenate([np.cos(angle), -np.sin(angle)], axis=1))


def depth_tables():
    device = np.arange(DEVICES)
    kz = reverse_bits(2 * device, 9)
    q, g, zh = np.meshgrid(np.arange(LAYERS), np.arange(GROUPS), np.arange(8), indexing="ij")
    tables = []
    for parity in range(2):
        z = (g * 64 + q * 16 + 2 * zh + parity).reshape(-1)
        angle = 2.0 * np.pi * (kz[:, None] * z[None, :] % NZ) / NZ
        cos, sin = np.cos(angle), np.sin(angle)
        tables.append(np.block([[cos, sin], [-sin, cos]]))
    return halves_np(np.stack(tables))


def cell_tables():
    yy, xx = np.divmod(np.arange(DEVICES), BRICK)

    def block(k1y, k1x):
        angle = 2.0 * np.pi * ((k1y[:, None] * yy + k1x[:, None] * xx) % BRICK) / BRICK
        cos, sin = np.cos(angle), np.sin(angle)
        return np.block([[cos, sin], [-sin, cos]])

    t, j, k1x = (a.reshape(-1) for a in np.meshgrid(np.arange(4), np.arange(4), np.arange(8), indexing="ij"))
    main = block(4 * t + j, k1x)
    j, t = (a.reshape(-1) for a in np.meshgrid(np.arange(4), np.arange(8), indexing="ij"))
    last = block(4 * (t % 4) + j, np.full(32, 8))
    return halves_np(np.concatenate([main, last], axis=0))


def lap_tables():
    along_x = 4.0 * np.sin(np.pi * np.arange(288) / PLANE) ** 2
    along_y = 4.0 * np.sin(np.pi * np.arange(PLANE) / PLANE) ** 2
    rows = along_x[:256].reshape(8, 32).T
    lap_x = np.broadcast_to(rows[:, :, None], (32, 8, 128)).astype(np.float32)
    lap_y = np.broadcast_to(along_y.reshape(4, 1, 128), (4, 8, 128)).astype(np.float32)
    return lap_x, lap_y


def split(values):
    high = values.astype(BF16)
    return high, (values - high.astype(F32)).astype(BF16)


def dot(a, b):
    return jnp.dot(a, b, preferred_element_type=F32)


def dot3(a_high, a_low, b_high, b_low):
    return dot(a_high, b_high) + dot(a_high, b_low) + dot(a_low, b_high)


def middle_kernel(
    cells, places, twiddle, lat_high, lat_low, dep_high, dep_low, out, field_high, field_low
):
    lane_group = lax.broadcasted_iota(jnp.int32, (8, DEVICES), 1) // 32
    site = lax.broadcasted_iota(jnp.int32, (DEVICES, SITES), 1).astype(F32)

    def place_layer(q, _):
        where = places[q]
        total = jnp.zeros((256, SITES), F32)
        for c in range(CAP):
            rows = []
            for parity in range(2):
                at = pl.multiple_of(q * 256 + c * 16 + parity * 8, 8)
                rows.append(cells[pl.ds(at, 8), :])
            tops = [r.astype(BF16).astype(F32) for r in rows]
            lows = [r - t for r, t in zip(rows, tops)]
            pieces = [
                jnp.where(lane_group == g, part, 0.0)
                for part in tops + lows
                for g in range(GROUPS)
            ]
            spread = jnp.concatenate(pieces, axis=0).astype(BF16)
            chosen = jnp.where(where[:, c : c + 1] == site, 1.0, 0.0).astype(BF16)
            total = total + dot(spread, chosen)
        layer = total[:128] + total[128:]
        high, low = split(layer)
        for parity in range(2):
            at = pl.multiple_of(parity * 256 + q * 64, 64)
            field_high[pl.ds(at, 64), :] = high[parity * 64 : parity * 64 + 64]
            field_low[pl.ds(at, 64), :] = low[parity * 64 : parity * 64 + 64]
        return 0

    lax.fori_loop(0, LAYERS, place_layer, 0)

    def columns(tile, _):
        at = pl.multiple_of(tile * 256, 256)
        parts = []
        for ri in range(2):
            from_col = pl.ds(pl.multiple_of(ri * SITES + at, 256), 256)
            parts.append(
                dot3(
                    field_high[...], field_low[...], lat_high[:, from_col], lat_low[:, from_col]
                )
            )
        turn_re = twiddle[0:1, pl.ds(at, 256)]
        turn_im = twiddle[1:2, pl.ds(at, 256)]
        real = parts[0] * turn_re - parts[1] * turn_im
        imag = parts[0] * turn_im + parts[1] * turn_re
        sums = []
        for parity in range(2):
            rows = slice(parity * 256, parity * 256 + 256)
            high, low = split(jnp.concatenate([real[rows], imag[rows]], axis=0))
            sums.append(dot3(dep_high[parity], dep_low[parity], high, low))
        for b in range(2):
            both = sums[0] + sums[1] if b == 0 else sums[0] - sums[1]
            for ri in range(2):
                for h in range(2):
                    out[pl.ds((b * 2 + ri) * 8 + tile * 2 + h, DEVICES, stride=32), :] = both[
                        ri * 256 : ri * 256 + 256, h * 128 : h * 128 + 128
                    ]
        return 0

    lax.fori_loop(0, SITES // 256, columns, 0)


def middle(cells, places, twiddle):
    tables = [jnp.asarray(t) for t in (*lattice_tables(), *depth_tables())]
    return pl.pallas_call(
        middle_kernel,
        out_shape=jax.ShapeDtypeStruct((DEVICES * 32, 128), F32),
        in_specs=[pl.BlockSpec(memory_space=pltpu.VMEM)] * 7,
        out_specs=pl.BlockSpec(memory_space=pltpu.VMEM),
        scratch_shapes=[pltpu.VMEM((NZ, SITES), BF16), pltpu.VMEM((NZ, SITES), BF16)],
        compiler_params=pltpu.CompilerParams(vmem_limit_bytes=56 << 20),
        name="middle",
    )(cells, places, twiddle, *tables)


def final_kernel(pieces, lap_z, lap_x, lap_y, cell_high, cell_low, out_re, out_im, rows_ref):
    block = lax.broadcasted_iota(jnp.int32, (8, 128), 1) // 32
    scale = -1.0 / math.sqrt(PLANE * PLANE * NZ)
    outs = (out_re, out_im)

    def group(step, _):
        b = step // 4
        pair = step % 4
        parts = []
        for ri in range(2):
            halves = [
                pieces[pl.ds((b * 2 + ri) * 8 + pair * 2 + h, DEVICES, stride=32), :]
                for h in range(2)
            ]
            parts.append(jnp.concatenate(halves, axis=1))
        high, low = split(jnp.concatenate(parts, axis=0))
        result = dot3(cell_high[0:256, :], cell_low[0:256, :], high, low)
        along_z = lap_z[b]
        for h in range(2):
            for t in range(4):
                tiles = []
                for ri in range(2):
                    at = ri * 128 + t * 32
                    row = [
                        result[at + j * 8 : at + j * 8 + 8, h * 128 : h * 128 + 128]
                        for j in range(4)
                    ]
                    tiles.append(transpose_blocks(row, block))
                for r in range(4):
                    kx = (pair * 2 + h) * 4 + r
                    factor = scale / (along_z + lap_x[kx] + lap_y[t] + SCREEN)
                    for ri in range(2):
                        rows_ref[pl.ds((ri * 4 + t) * 256 + kx, 8, stride=32), :] = (
                            tiles[ri][r] * factor
                        )

        @pl.when(pair == 0)
        def _():
            last = dot3(cell_high[256:320, :], cell_low[256:320, :], high[:, :128], low[:, :128])
            for ri in range(2):
                line = jnp.zeros((8, 128), F32)
                for j in range(4):
                    part = last[ri * 32 + j * 8 : ri * 32 + j * 8 + 8, :]
                    moved = part if j == 0 else pltpu.roll(part, 32 * j, 1)
                    line = jnp.where(block == j, moved, line)
                for t in range(4):
                    factor = scale / (along_z[0:1] + 4.0 + lap_y[t, 0:1] + SCREEN)
                    outs[ri][b, 256:257, t * 128 : t * 128 + 128] = line[t : t + 1] * factor

        @pl.when(pair == 3)
        def _():
            for ri in range(2):
                for t in range(4):
                    at = (ri * 4 + t) * 256
                    outs[ri][b, 0:256, t * 128 : t * 128 + 128] = rows_ref[at : at + 256, :]

        return 0

    lax.fori_loop(0, 8, group, 0)


def transpose_blocks(row, block):
    tiles = []
    for r in range(4):
        tile = row[r]
        for j in range(4):
            if j != r:
                tile = jnp.where(block == j, pltpu.roll(row[j], (32 * (j - r)) % 128, 1), tile)
        tiles.append(tile)
    return tiles


def final(pieces, lap_z):
    lap_x, lap_y = lap_tables()
    tables = [jnp.asarray(t) for t in (lap_x, lap_y, *cell_tables())]
    shape = jax.ShapeDtypeStruct((2, KX, PLANE), F32)
    return pl.pallas_call(
        final_kernel,
        out_shape=(shape, shape),
        in_specs=[pl.BlockSpec(memory_space=pltpu.VMEM)] * 6,
        out_specs=(pl.BlockSpec(memory_space=pltpu.VMEM), pl.BlockSpec(memory_space=pltpu.VMEM)),
        scratch_shapes=[pltpu.VMEM((8 * 256, 128), F32)],
        compiler_params=pltpu.CompilerParams(vmem_limit_bytes=56 << 20),
        name="final",
    )(pieces, lap_z, *tables)


def twiddle_of(device):
    yy = device // BRICK
    xx = device % BRICK
    column = jnp.arange(SITES, dtype=jnp.int32)
    turn = ((column // BLOCKS) * xx + (column % BLOCKS) * yy) % PLANE
    angle = (2.0 * math.pi / PLANE) * turn.astype(F32)
    return jnp.stack([jnp.cos(angle), -jnp.sin(angle)])


def lap_z_of(device):
    kz = reverse_bits(2 * device + jnp.arange(2, dtype=jnp.int32), 9)
    along_z = 4.0 * jnp.sin(math.pi * kz.astype(F32) / NZ) ** 2
    return jnp.broadcast_to(along_z[:, None, None], (2, 8, 128))


def on_device(brick_data, brick_xy, brick_live):
    device = lax.axis_index("zg") * 32 + lax.axis_index("zl")
    live = jnp.arange(CAP, dtype=jnp.int32)[None, :] < brick_live
    place = (brick_xy[0] * BLOCKS + brick_xy[1]).astype(F32).reshape(LAYERS, CAP)
    place = jnp.where(live, place, -1.0).reshape(SLOTS, 1)
    by_parity = jnp.swapaxes(brick_data.reshape(SLOTS, 8, 2, 256), 1, 2)
    outgoing = jnp.concatenate(
        [by_parity.reshape(SLOTS * BRICK, 256), jnp.broadcast_to(place, (SLOTS, 256))], axis=0
    )
    sent = outgoing.T.reshape(DEVICES, 1, SLOTS * (BRICK + 1))
    got = lax.all_to_all(sent, AXES, 0, 0, tiled=True).reshape(DEVICES, SLOTS * (BRICK + 1))
    cells = got[:, : SLOTS * BRICK].T
    places = got[:, SLOTS * BRICK :].reshape(DEVICES, LAYERS, CAP).transpose(1, 0, 2)
    rows = middle(cells, places, twiddle_of(device))
    pieces = lax.all_to_all(rows.reshape(DEVICES, 32, 128), AXES, 0, 0, tiled=True)
    return final(pieces.reshape(DEVICES * 32, 128), lap_z_of(device))


def solution(mesh):
    in_specs = (P(AXES, None, None), P(None, AXES), P(None, AXES))
    out_specs = (P(AXES, None, None), P(AXES, None, None))
    return jax.shard_map(
        on_device, mesh=mesh, in_specs=in_specs, out_specs=out_specs, check_vma=False
    )
```

```python
import math

import jax
import jax.numpy as jnp
import numpy as np
from jax import lax
from jax.experimental import pallas as pl
from jax.experimental.pallas import tpu as pltpu
from jax.sharding import PartitionSpec as P

AXES = ("zg", "zl")
NZ = 512
PLANE = 512
BRICK = 16
BLOCKS = 32
LAYERS = 4
CAP = 16
GROUPS = 8
DEVICES = 256
KX = 257
SLOTS = LAYERS * CAP
SITES = BLOCKS * BLOCKS
SCREEN = 0.25
CHUNK = 9
BF16 = jnp.bfloat16
F32 = jnp.float32


def reverse_bits(values, digits):
    result = values * 0
    for digit in range(digits):
        result = result | ((values >> digit) & 1) << (digits - 1 - digit)
    return result


def halves_np(table):
    high = table.astype(np.float32).astype(jnp.bfloat16)
    low = (table - high.astype(np.float64)).astype(np.float32).astype(jnp.bfloat16)
    return high, low


def lattice_tables():
    bx, by = np.divmod(np.arange(SITES), BLOCKS)
    kx, ky = np.divmod(np.arange(SITES), BLOCKS)
    turn = (bx[:, None] * kx[None, :] + by[:, None] * ky[None, :]) % BLOCKS
    angle = 2.0 * np.pi * turn / BLOCKS
    return halves_np(np.concatenate([np.cos(angle), -np.sin(angle)], axis=1))


def depth_tables():
    device = np.arange(DEVICES)
    kz = reverse_bits(2 * device, 9)
    q, g, zh = np.meshgrid(np.arange(LAYERS), np.arange(GROUPS), np.arange(8), indexing="ij")
    tables = []
    for parity in range(2):
        z = (g * 64 + q * 16 + 2 * zh + parity).reshape(-1)
        angle = 2.0 * np.pi * (kz[:, None] * z[None, :] % NZ) / NZ
        cos, sin = np.cos(angle), np.sin(angle)
        tables.append(np.block([[cos, sin], [-sin, cos]]))
    return halves_np(np.stack(tables))


def cell_tables():
    yy, xx = np.divmod(np.arange(DEVICES), BRICK)

    def block(k1y, k1x):
        angle = 2.0 * np.pi * ((k1y[:, None] * yy + k1x[:, None] * xx) % BRICK) / BRICK
        cos, sin = np.cos(angle), np.sin(angle)
        return np.block([[cos, sin], [-sin, cos]])

    t, j, k1x = (a.reshape(-1) for a in np.meshgrid(np.arange(4), np.arange(4), np.arange(8), indexing="ij"))
    main = block(4 * t + j, k1x)
    j, t = (a.reshape(-1) for a in np.meshgrid(np.arange(4), np.arange(8), indexing="ij"))
    last = block(4 * (t % 4) + j, np.full(32, 8))
    return halves_np(np.concatenate([main, last], axis=0))


def lap_tables():
    along_x = 4.0 * np.sin(np.pi * np.arange(288) / PLANE) ** 2
    along_y = 4.0 * np.sin(np.pi * np.arange(PLANE) / PLANE) ** 2
    rows = along_x[:256].reshape(8, 32).T
    lap_x = np.broadcast_to(rows[:, :, None], (32, 8, 128)).astype(np.float32)
    lap_y = np.broadcast_to(along_y.reshape(4, 1, 128), (4, 8, 128)).astype(np.float32)
    return lap_x, lap_y


def split(values):
    high = values.astype(BF16)
    return high, (values - high.astype(F32)).astype(BF16)


def dot(a, b):
    return jnp.dot(a, b, preferred_element_type=F32)


def dot3(a_high, a_low, b_high, b_low):
    return dot(a_high, b_high) + dot(a_high, b_low) + dot(a_low, b_high)


def send_kernel(bricks, place, out):
    for h in range(2):
        for i in range(8):
            block = bricks[i * 128 : i * 128 + 128, h * 128 : h * 128 + 128]
            out[pl.ds(h * 128 * CHUNK + i, 128, stride=CHUNK), :] = block.T
    out[pl.ds(8, DEVICES, stride=CHUNK), :] = jnp.broadcast_to(place[...], (DEVICES, 128))


def send(bricks, place):
    return pl.pallas_call(
        send_kernel,
        out_shape=jax.ShapeDtypeStruct((DEVICES * CHUNK, 128), F32),
        in_specs=[pl.BlockSpec(memory_space=pltpu.VMEM)] * 2,
        out_specs=pl.BlockSpec(memory_space=pltpu.VMEM),
        compiler_params=pltpu.CompilerParams(vmem_limit_bytes=56 << 20),
        name="send",
    )(bricks, place)


def middle_kernel(
    got, twiddle, lat_high, lat_low, dep_high, dep_low, out, field_high, field_low, cells, places
):
    lane_group = lax.broadcasted_iota(jnp.int32, (8, 128), 1) // 32
    none = jnp.zeros((8, 128), F32)
    for i in range(8):
        block = got[pl.ds(i, DEVICES, stride=CHUNK), :].T
        for h in range(2):
            at = h * 1024 + i * 128
            cells[at : at + 128, :] = block[:, h * 128 : h * 128 + 128]
    codes = got[pl.ds(8, DEVICES, stride=CHUNK), :]
    for q in range(LAYERS):
        places[q] = codes if q == 0 else pltpu.roll(codes, 128 - q * CAP, 1)
    site = lax.broadcasted_iota(jnp.int32, (DEVICES, SITES), 1).astype(F32)

    def place_layer(q, _):
        where = places[q]
        total = jnp.zeros((256, SITES), F32)
        for c in range(CAP):
            pieces = {}
            for parity in range(2):
                for h in range(2):
                    row = cells[pl.ds(h * 1024 + q * 256 + c * 16 + parity, 8, stride=2), :]
                    top = row.astype(BF16).astype(F32)
                    pieces[0, parity, h] = top
                    pieces[1, parity, h] = row - top
            spread = []
            for part in range(2):
                for parity in range(2):
                    for g in range(GROUPS):
                        own = jnp.where(lane_group == g % 4, pieces[part, parity, g // 4], 0.0)
                        pair = [own, none] if g < 4 else [none, own]
                        spread.append(jnp.concatenate(pair, axis=1))
            spread = jnp.concatenate(spread, axis=0).astype(BF16)
            chosen = jnp.where(where[:, c : c + 1] == site, 1.0, 0.0).astype(BF16)
            total = total + dot(spread, chosen)
        layer = total[:128] + total[128:]
        high, low = split(layer)
        for parity in range(2):
            at = pl.multiple_of(parity * 256 + q * 64, 64)
            field_high[pl.ds(at, 64), :] = high[parity * 64 : parity * 64 + 64]
            field_low[pl.ds(at, 64), :] = low[parity * 64 : parity * 64 + 64]
        return 0

    lax.fori_loop(0, LAYERS, place_layer, 0)

    def columns(tile, _):
        at = pl.multiple_of(tile * 256, 256)
        parts = []
        for ri in range(2):
            from_col = pl.ds(pl.multiple_of(ri * SITES + at, 256), 256)
            parts.append(
                dot3(
                    field_high[...], field_low[...], lat_high[:, from_col], lat_low[:, from_col]
                )
            )
        turn_re = twiddle[0:1, pl.ds(at, 256)]
        turn_im = twiddle[1:2, pl.ds(at, 256)]
        real = parts[0] * turn_re - parts[1] * turn_im
        imag = parts[0] * turn_im + parts[1] * turn_re
        sums = []
        for parity in range(2):
            rows = slice(parity * 256, parity * 256 + 256)
            high, low = split(jnp.concatenate([real[rows], imag[rows]], axis=0))
            sums.append(dot3(dep_high[parity], dep_low[parity], high, low))
        for b in range(2):
            both = sums[0] + sums[1] if b == 0 else sums[0] - sums[1]
            for ri in range(2):
                for h in range(2):
                    out[pl.ds((b * 2 + ri) * 8 + tile * 2 + h, DEVICES, stride=32), :] = both[
                        ri * 256 : ri * 256 + 256, h * 128 : h * 128 + 128
                    ]
        return 0

    lax.fori_loop(0, SITES // 256, columns, 0)


def middle(got, twiddle):
    tables = [jnp.asarray(t) for t in (*lattice_tables(), *depth_tables())]
    return pl.pallas_call(
        middle_kernel,
        out_shape=jax.ShapeDtypeStruct((DEVICES * 32, 128), F32),
        in_specs=[pl.BlockSpec(memory_space=pltpu.VMEM)] * 6,
        out_specs=pl.BlockSpec(memory_space=pltpu.VMEM),
        scratch_shapes=[
            pltpu.VMEM((NZ, SITES), BF16),
            pltpu.VMEM((NZ, SITES), BF16),
            pltpu.VMEM((2 * SLOTS * BRICK, 128), F32),
            pltpu.VMEM((LAYERS, DEVICES, 128), F32),
        ],
        compiler_params=pltpu.CompilerParams(vmem_limit_bytes=56 << 20),
        name="middle",
    )(got, twiddle, *tables)


def final_kernel(pieces, lap_z, lap_x, lap_y, cell_high, cell_low, out_re, out_im):
    block = lax.broadcasted_iota(jnp.int32, (8, 128), 1) // 32
    scale = -1.0 / math.sqrt(PLANE * PLANE * NZ)
    outs = (out_re, out_im)

    def group(step, _):
        b = step // 4
        pair = step % 4
        parts = []
        for ri in range(2):
            halves = [
                pieces[pl.ds((b * 2 + ri) * 8 + pair * 2 + h, DEVICES, stride=32), :]
                for h in range(2)
            ]
            parts.append(jnp.concatenate(halves, axis=1))
        high, low = split(jnp.concatenate(parts, axis=0))
        result = dot3(cell_high[0:256, :], cell_low[0:256, :], high, low)
        along_z = lap_z[b]
        for h in range(2):
            for t in range(4):
                tiles = []
                for ri in range(2):
                    at = ri * 128 + t * 32
                    row = [
                        result[at + j * 8 : at + j * 8 + 8, h * 128 : h * 128 + 128]
                        for j in range(4)
                    ]
                    tiles.append(transpose_blocks(row, block))
                for r in range(4):
                    kx = (pair * 2 + h) * 4 + r
                    factor = scale / (along_z + lap_x[kx] + lap_y[t] + SCREEN)
                    for ri in range(2):
                        outs[ri][pl.ds(kx * 8 + t * 2 + b, 8, stride=256), :] = tiles[ri][r] * factor

        @pl.when(pair == 0)
        def _():
            last = dot3(cell_high[256:320, :], cell_low[256:320, :], high[:, :128], low[:, :128])
            for ri in range(2):
                line = jnp.zeros((8, 128), F32)
                for j in range(4):
                    part = last[ri * 32 + j * 8 : ri * 32 + j * 8 + 8, :]
                    moved = part if j == 0 else pltpu.roll(part, 32 * j, 1)
                    line = jnp.where(block == j, moved, line)
                for t in range(4):
                    factor = scale / (along_z[0:1] + 4.0 + lap_y[t, 0:1] + SCREEN)
                    outs[ri][pl.ds(2048 + t * 2 + b, 1), :] = line[t : t + 1] * factor

        return 0

    lax.fori_loop(0, 8, group, 0)


def transpose_blocks(row, block):
    tiles = []
    for r in range(4):
        tile = row[r]
        for j in range(4):
            if j != r:
                tile = jnp.where(block == j, pltpu.roll(row[j], (32 * (j - r)) % 128, 1), tile)
        tiles.append(tile)
    return tiles


def final(pieces, lap_z):
    lap_x, lap_y = lap_tables()
    tables = [jnp.asarray(t) for t in (lap_x, lap_y, *cell_tables())]
    shape = jax.ShapeDtypeStruct((KX * 8, 128), F32)
    outs = pl.pallas_call(
        final_kernel,
        out_shape=(shape, shape),
        in_specs=[pl.BlockSpec(memory_space=pltpu.VMEM)] * 6,
        out_specs=(pl.BlockSpec(memory_space=pltpu.VMEM), pl.BlockSpec(memory_space=pltpu.VMEM)),
        compiler_params=pltpu.CompilerParams(vmem_limit_bytes=56 << 20),
        name="final",
    )(pieces, lap_z, *tables)
    return tuple(
        o.reshape(KX, 4, 2, 128).transpose(2, 0, 1, 3).reshape(2, KX, PLANE) for o in outs
    )


def twiddle_of(device):
    yy = device // BRICK
    xx = device % BRICK
    column = jnp.arange(SITES, dtype=jnp.int32)
    turn = ((column // BLOCKS) * xx + (column % BLOCKS) * yy) % PLANE
    angle = (2.0 * math.pi / PLANE) * turn.astype(F32)
    return jnp.stack([jnp.cos(angle), -jnp.sin(angle)])


def lap_z_of(device):
    kz = reverse_bits(2 * device + jnp.arange(2, dtype=jnp.int32), 9)
    along_z = 4.0 * jnp.sin(math.pi * kz.astype(F32) / NZ) ** 2
    return jnp.broadcast_to(along_z[:, None, None], (2, 8, 128))


def on_device(brick_data, brick_xy, brick_live):
    device = lax.axis_index("zg") * 32 + lax.axis_index("zl")
    live = jnp.arange(CAP, dtype=jnp.int32)[None, :] < brick_live
    place = (brick_xy[0] * BLOCKS + brick_xy[1]).astype(F32).reshape(LAYERS, CAP)
    place = jnp.where(live, place, -1.0).reshape(1, SLOTS)
    place = jnp.pad(place, ((0, 0), (0, 128 - SLOTS)))
    sent = send(brick_data.reshape(SLOTS * BRICK, 256), place)
    got = lax.all_to_all(sent.reshape(DEVICES, 1, CHUNK * 128), AXES, 0, 0, tiled=True)
    rows = middle(got.reshape(DEVICES * CHUNK, 128), twiddle_of(device))
    pieces = lax.all_to_all(rows.reshape(DEVICES, 32, 128), AXES, 0, 0, tiled=True)
    return final(pieces.reshape(DEVICES * 32, 128), lap_z_of(device))


def solution(mesh):
    in_specs = (P(AXES, None, None), P(None, AXES), P(None, AXES))
    out_specs = (P(AXES, None, None), P(AXES, None, None))
    return jax.shard_map(
        on_device, mesh=mesh, in_specs=in_specs, out_specs=out_specs, check_vma=False
    )
```

```python
import math

import jax
import jax.numpy as jnp
import numpy as np
from jax import lax
from jax.experimental import pallas as pl
from jax.experimental.pallas import tpu as pltpu
from jax.sharding import PartitionSpec as P

AXES = ("zg", "zl")
NZ = 512
PLANE = 512
BRICK = 16
BLOCKS = 32
LAYERS = 4
CAP = 16
GROUPS = 8
DEVICES = 256
KX = 257
SLOTS = LAYERS * CAP
SITES = BLOCKS * BLOCKS
SCREEN = 0.25
TOGETHER = 4
CHUNK = 9
BF16 = jnp.bfloat16
F32 = jnp.float32


def reverse_bits(values, digits):
    result = values * 0
    for digit in range(digits):
        result = result | ((values >> digit) & 1) << (digits - 1 - digit)
    return result


def halves_np(table):
    high = table.astype(np.float32).astype(jnp.bfloat16)
    low = (table - high.astype(np.float64)).astype(np.float32).astype(jnp.bfloat16)
    return high, low


def lattice_tables():
    inner, by = np.divmod(np.arange(256), BLOCKS)
    k_high, ky = np.divmod(np.arange(256), BLOCKS)
    tables = []
    for k_low in range(4):
        turn = inner[:, None] * (k_low + 4 * k_high)[None, :] + by[:, None] * ky[None, :]
        angle = 2.0 * np.pi * (turn % BLOCKS) / BLOCKS
        real, imag = np.cos(angle), -np.sin(angle)
        if k_low == 1:
            below = [imag, -real]
        elif k_low == 3:
            below = [-imag, real]
        else:
            below = [0.0 * real, 0.0 * real]
        tables.append(np.block([[real, imag], below]))
    return halves_np(np.stack(tables))


def depth_tables():
    device = np.arange(DEVICES)
    kz = reverse_bits(2 * device, 9)
    q, g, zh = np.meshgrid(np.arange(LAYERS), np.arange(GROUPS), np.arange(8), indexing="ij")
    tables = []
    for parity in range(2):
        z = (g * 64 + q * 16 + 2 * zh + parity).reshape(-1)
        angle = 2.0 * np.pi * (kz[:, None] * z[None, :] % NZ) / NZ
        cos, sin = np.cos(angle), np.sin(angle)
        tables.append(np.block([[cos, sin], [-sin, cos]]))
    return halves_np(np.stack(tables))


def cell_tables():
    yy, xx = np.divmod(np.arange(DEVICES), BRICK)

    def block(k1y, k1x):
        angle = 2.0 * np.pi * ((k1y[:, None] * yy + k1x[:, None] * xx) % BRICK) / BRICK
        cos, sin = np.cos(angle), np.sin(angle)
        return np.block([[cos, sin], [-sin, cos]])

    t, j, k1x = (a.reshape(-1) for a in np.meshgrid(np.arange(4), np.arange(4), np.arange(8), indexing="ij"))
    main = block(4 * t + j, k1x)
    j, t = (a.reshape(-1) for a in np.meshgrid(np.arange(4), np.arange(8), indexing="ij"))
    last = block(4 * (t % 4) + j, np.full(32, 8))
    return halves_np(np.concatenate([main, last], axis=0))


def lap_tables():
    along_x = 4.0 * np.sin(np.pi * np.arange(288) / PLANE) ** 2
    along_y = 4.0 * np.sin(np.pi * np.arange(PLANE) / PLANE) ** 2
    rows = along_x[:256].reshape(8, 32).T
    lap_x = np.broadcast_to(rows[:, :, None], (32, 8, 128)).astype(np.float32)
    lap_y = np.broadcast_to(along_y.reshape(4, 1, 128), (4, 8, 128)).astype(np.float32)
    return lap_x, lap_y


def split(values):
    high = values.astype(BF16)
    return high, (values - high.astype(F32)).astype(BF16)


def dot(a, b):
    return jnp.dot(a, b, preferred_element_type=F32)


def dot3(a_high, a_low, b_high, b_low):
    return dot(a_high, b_high) + dot(a_high, b_low) + dot(a_low, b_high)


def send_kernel(bricks, xy, live, out):
    for h in range(2):
        for i in range(8):
            block = bricks[i * 128 : i * 128 + 128, h * 128 : h * 128 + 128]
            out[pl.ds(h * 128 * CHUNK + i, 128, stride=CHUNK), :] = block.T
    slot = lax.broadcasted_iota(jnp.int32, (1, SLOTS), 1)
    count = jnp.zeros((1, SLOTS), jnp.int32)
    for q in range(LAYERS):
        count = jnp.where(slot // CAP == q, live[0, q], count)
    place = jnp.where(slot % CAP < count, xy[0:1, :] * BLOCKS + xy[1:2, :], -1)
    place = jnp.concatenate([place, jnp.full((1, 128 - SLOTS), -1, jnp.int32)], axis=1)
    out[pl.ds(8, DEVICES, stride=CHUNK), :] = jnp.broadcast_to(place.astype(F32), (DEVICES, 128))


def send(bricks, xy, live):
    return pl.pallas_call(
        send_kernel,
        out_shape=jax.ShapeDtypeStruct((DEVICES * CHUNK, 128), F32),
        in_specs=[
            pl.BlockSpec(memory_space=pltpu.VMEM),
            pl.BlockSpec(memory_space=pltpu.VMEM),
            pl.BlockSpec(memory_space=pltpu.SMEM),
        ],
        out_specs=pl.BlockSpec(memory_space=pltpu.VMEM),
        compiler_params=pltpu.CompilerParams(vmem_limit_bytes=56 << 20),
        name="send",
    )(bricks, xy, live)


def read_cells(got, cells, places):
    for i in range(8):
        block = got[pl.ds(i, DEVICES, stride=CHUNK), :].T
        for h in range(2):
            at = h * 1024 + i * 128
            cells[at : at + 128, :] = block[:, h * 128 : h * 128 + 128]
    codes = got[pl.ds(8, DEVICES, stride=CHUNK), :]
    for q in range(LAYERS):
        places[q] = codes if q == 0 else pltpu.roll(codes, 128 - q * CAP, 1)


def spread_cells(cells, q, c, h, lane_group):
    tops, lows = [], []
    for parity in range(2):
        row = cells[pl.ds(h * 1024 + q * 256 + c * 16 + parity, 8, stride=2), :]
        tops.append(row.astype(BF16).astype(F32))
        lows.append(row - tops[-1])
    spread = [jnp.where(lane_group == g, piece, 0.0) for piece in tops + lows for g in range(4)]
    return jnp.concatenate(spread, axis=0).astype(BF16)


def place_layers(cells, places, field_high, field_low):
    lane_group = lax.broadcasted_iota(jnp.int32, (8, 128), 1) // 32
    site = lax.broadcasted_iota(jnp.int32, (128, SITES), 1).astype(F32)

    def place_layer(q, _):
        for h in range(2):
            where = places[q, h * 128 : h * 128 + 128, :]
            total = None
            for first in range(0, CAP, TOGETHER):
                slots = range(first, first + TOGETHER)
                spread = [spread_cells(cells, q, c, h, lane_group) for c in slots]
                chosen = [jnp.where(where[:, c : c + 1] == site, 1.0, 0.0).astype(BF16) for c in slots]
                part = dot(jnp.concatenate(spread, axis=1), jnp.concatenate(chosen, axis=0))
                total = part if total is None else total + part
            layer = total[:64] + total[64:]
            x = [layer[:, k * 256 : k * 256 + 256] for k in range(4)]
            even, odd = x[0] + x[2], x[1] + x[3]
            high, low = split(
                jnp.concatenate([even + odd, even - odd, x[0] - x[2], x[1] - x[3]], axis=1)
            )
            for parity in range(2):
                at = pl.multiple_of(parity * 256 + q * 64 + h * 32, 32)
                field_high[pl.ds(at, 32), :] = high[parity * 32 : parity * 32 + 32]
                field_low[pl.ds(at, 32), :] = low[parity * 32 : parity * 32 + 32]
        return 0

    lax.fori_loop(0, LAYERS, place_layer, 0)


def middle_kernel(
    got_any, twiddle, lat_high, lat_low, dep_any, out, got, dep, field_high, field_low, cells, places, spec, sems
):
    step = pl.program_id(0)

    @pl.when(step == 0)
    def _():
        fetch_dep = pltpu.make_async_copy(dep_any, dep, sems.at[1])
        fetch_dep.start()
        fetch_got = pltpu.make_async_copy(got_any, got, sems.at[0])
        fetch_got.start()
        fetch_got.wait()
        read_cells(got, cells, places)
        place_layers(cells, places, field_high, field_low)
        fetch_dep.wait()

    for even in range(2):
        @pl.when((step == 0) | (step == 2) if even else (step == 1) | (step == 3))
        def _(even=even):
            if even:
                at = pl.multiple_of(step * 128, 256)
                from_cols, rows = pl.ds(at, 256), slice(0, 256)
            else:
                from_cols, rows = pl.ds(512, 512), slice(0, 512)
            spec[...] = dot3(
                field_high[:, from_cols], field_low[:, from_cols], lat_high[0, rows, :], lat_low[0, rows, :]
            )

    turn_re = twiddle[0:1, :]
    turn_im = twiddle[1:2, :]
    real = spec[:, 0:256] * turn_re - spec[:, 256:512] * turn_im
    imag = spec[:, 0:256] * turn_im + spec[:, 256:512] * turn_re
    sums = []
    for parity in range(2):
        rows = slice(parity * 256, parity * 256 + 256)
        high, low = split(jnp.concatenate([real[rows], imag[rows]], axis=0))
        sums.append(dot3(dep[0, parity], dep[1, parity], high, low))
    flat = out.reshape(DEVICES * 8, 128)
    for b in range(2):
        both = sums[0] + sums[1] if b == 0 else sums[0] - sums[1]
        for ri in range(2):
            for h in range(2):
                flat[pl.ds((b * 2 + ri) * 2 + h, DEVICES, stride=8), :] = both[
                    ri * 256 : ri * 256 + 256, h * 128 : h * 128 + 128
                ]


def middle(got, twiddle):
    lat_high, lat_low = (jnp.asarray(t) for t in lattice_tables())
    dep = jnp.asarray(np.stack(depth_tables()))
    whole = pl.BlockSpec(memory_space=pl.ANY)
    quarter = pl.BlockSpec((1, 512, 512), lambda step: (step, 0, 0))
    return pl.pallas_call(
        middle_kernel,
        grid=(4,),
        out_shape=jax.ShapeDtypeStruct((DEVICES, 32, 128), F32),
        in_specs=[whole, pl.BlockSpec((2, 256), lambda step: (0, step)), quarter, quarter, whole],
        out_specs=pl.BlockSpec((DEVICES, 8, 128), lambda step: (0, step, 0)),
        scratch_shapes=[
            pltpu.VMEM((DEVICES * CHUNK, 128), F32),
            pltpu.VMEM(dep.shape, BF16),
            pltpu.VMEM((NZ, SITES), BF16),
            pltpu.VMEM((NZ, SITES), BF16),
            pltpu.VMEM((2 * SLOTS * BRICK, 128), F32),
            pltpu.VMEM((LAYERS, DEVICES, 128), F32),
            pltpu.VMEM((NZ, 512), F32),
            pltpu.SemaphoreType.DMA((2,)),
        ],
        compiler_params=pltpu.CompilerParams(vmem_limit_bytes=56 << 20),
        name="middle",
    )(got, twiddle, lat_high, lat_low, dep)


def final_kernel(pieces, lap_z, lap_x, lap_y, cell_high, cell_low, out_re, out_im):
    step = pl.program_id(0)
    block = lax.broadcasted_iota(jnp.int32, (8, 128), 1) // 32
    scale = -1.0 / math.sqrt(PLANE * PLANE * NZ)
    outs = (out_re, out_im)
    flat = pieces.reshape(DEVICES * 8, 128)
    for b in range(2):
        parts = []
        for ri in range(2):
            halves = [flat[pl.ds((b * 2 + ri) * 2 + h, DEVICES, stride=8), :] for h in range(2)]
            parts.append(jnp.concatenate(halves, axis=1))
        high, low = split(jnp.concatenate(parts, axis=0))
        result = dot3(cell_high[0:256, :], cell_low[0:256, :], high, low)
        along_z = lap_z[b]
        for h in range(2):
            along_x = [lap_x[step + 16 * h + 4 * r] + (along_z + SCREEN) for r in range(4)]
            for t in range(4):
                tiles = []
                for ri in range(2):
                    at = ri * 128 + t * 32
                    row = [
                        result[at + j * 8 : at + j * 8 + 8, h * 128 : h * 128 + 128]
                        for j in range(4)
                    ]
                    tiles.append(transpose_blocks(row, block))
                for r in range(4):
                    kx = step + 16 * h + 4 * r
                    factor = scale / (along_x[r] + lap_y[t])
                    for ri in range(2):
                        outs[ri][pl.ds(kx * 8 + t * 2 + b, 8, stride=256), :] = tiles[ri][r] * factor

        @pl.when(step == 0)
        def _():
            last = dot3(cell_high[256:320, :], cell_low[256:320, :], high[:, :128], low[:, :128])
            for ri in range(2):
                line = jnp.zeros((8, 128), F32)
                for j in range(4):
                    part = last[ri * 32 + j * 8 : ri * 32 + j * 8 + 8, :]
                    moved = part if j == 0 else pltpu.roll(part, 32 * j, 1)
                    line = jnp.where(block == j, moved, line)
                for t in range(4):
                    factor = scale / (along_z + 4.0 + lap_y[t, 0:1] + SCREEN)
                    outs[ri][2048 + t * 2 + b : 2049 + t * 2 + b, :] = line[t : t + 1] * factor


def transpose_blocks(row, block):
    tiles = []
    for r in range(4):
        tile = row[r]
        for j in range(4):
            if j != r:
                tile = jnp.where(block == j, pltpu.roll(row[j], (32 * (j - r)) % 128, 1), tile)
        tiles.append(tile)
    return tiles


def final(pieces, lap_z):
    lap_x, lap_y = lap_tables()
    tables = [jnp.asarray(t) for t in (lap_x, lap_y, *cell_tables())]
    shape = jax.ShapeDtypeStruct((KX * 8, 128), F32)
    vmem = pl.BlockSpec(memory_space=pltpu.VMEM)
    rows = pl.BlockSpec((KX * 8, 128), lambda step: (0, 0))
    outs = pl.pallas_call(
        final_kernel,
        grid=(4,),
        out_shape=(shape, shape),
        in_specs=[
            pl.BlockSpec((DEVICES, 8, 128), lambda step: (0, step, 0)),
            pl.BlockSpec(memory_space=pltpu.SMEM),
            vmem,
            vmem,
            vmem,
            vmem,
        ],
        out_specs=(rows, rows),
        compiler_params=pltpu.CompilerParams(vmem_limit_bytes=24 << 20),
        name="final",
    )(pieces, lap_z, *tables)
    return tuple(
        o.reshape(KX, 4, 2, 128).transpose(2, 0, 1, 3).reshape(2, KX, PLANE) for o in outs
    )


def twiddle_of(device):
    yy = device // BRICK
    xx = device % BRICK
    column = jnp.arange(SITES, dtype=jnp.int32)
    kx = column // 256 + 4 * (column % 256 // BLOCKS)
    turn = (kx * xx + (column % BLOCKS) * yy) % PLANE
    angle = (2.0 * math.pi / PLANE) * turn.astype(F32)
    return jnp.stack([jnp.cos(angle), -jnp.sin(angle)])


def lap_z_of(device):
    kz = reverse_bits(2 * device + jnp.arange(2, dtype=jnp.int32), 9)
    return 4.0 * jnp.sin(math.pi * kz.astype(F32) / NZ) ** 2


def on_device(brick_data, brick_xy, brick_live):
    device = lax.axis_index("zg") * 32 + lax.axis_index("zl")
    sent = send(brick_data.reshape(SLOTS * BRICK, 256), brick_xy, brick_live.T)
    got = lax.all_to_all(sent.reshape(DEVICES, 1, CHUNK * 128), AXES, 0, 0, tiled=True)
    rows = middle(got.reshape(DEVICES * CHUNK, 128), twiddle_of(device))
    pieces = lax.all_to_all(rows, AXES, 0, 0, tiled=True)
    return final(pieces, lap_z_of(device))


def solution(mesh):
    in_specs = (P(AXES, None, None), P(None, AXES), P(None, AXES))
    out_specs = (P(AXES, None, None), P(AXES, None, None))
    return jax.shard_map(
        on_device, mesh=mesh, in_specs=in_specs, out_specs=out_specs, check_vma=False
    )
```

```python
import math

import jax
import jax.numpy as jnp
import numpy as np
from jax import lax
from jax.experimental import pallas as pl
from jax.experimental.pallas import tpu as pltpu
from jax.sharding import PartitionSpec as P

AXES = ("zg", "zl")
NZ = 512
PLANE = 512
BRICK = 16
BLOCKS = 32
LAYERS = 4
CAP = 16
GROUPS = 8
DEVICES = 256
KX = 257
SLOTS = LAYERS * CAP
SITES = BLOCKS * BLOCKS
SCREEN = 0.25
FETCHED = 2
TOGETHER = 4
CHUNK = 9
BF16 = jnp.bfloat16
F32 = jnp.float32


def reverse_bits(values, digits):
    result = values * 0
    for digit in range(digits):
        result = result | ((values >> digit) & 1) << (digits - 1 - digit)
    return result


def halves_np(table):
    high = table.astype(np.float32).astype(jnp.bfloat16)
    low = (table - high.astype(np.float64)).astype(np.float32).astype(jnp.bfloat16)
    return high, low


def lattice_tables():
    inner, by = np.divmod(np.arange(256), BLOCKS)
    k_high, ky = np.divmod(np.arange(256), BLOCKS)
    tables = []
    for k_low in range(4):
        turn = inner[:, None] * (k_low + 4 * k_high)[None, :] + by[:, None] * ky[None, :]
        angle = 2.0 * np.pi * (turn % BLOCKS) / BLOCKS
        real, imag = np.cos(angle), -np.sin(angle)
        if k_low == 1:
            below = [imag, -real]
        elif k_low == 3:
            below = [-imag, real]
        else:
            below = [0.0 * real, 0.0 * real]
        tables.append(np.block([[real, imag], below]))
    return halves_np(np.stack(tables))


def depth_tables():
    device = np.arange(DEVICES)
    kz = reverse_bits(2 * device, 9)
    q, g, zh = np.meshgrid(np.arange(LAYERS), np.arange(GROUPS), np.arange(8), indexing="ij")
    tables = []
    for parity in range(2):
        z = (g * 64 + q * 16 + 2 * zh + parity).reshape(-1)
        angle = 2.0 * np.pi * (kz[:, None] * z[None, :] % NZ) / NZ
        cos, sin = np.cos(angle), np.sin(angle)
        tables.append(np.block([[cos, sin], [-sin, cos]]))
    return halves_np(np.stack(tables))


def cell_tables():
    yy, xx = np.divmod(np.arange(DEVICES), BRICK)

    def block(k1y, k1x):
        angle = 2.0 * np.pi * ((k1y[:, None] * yy + k1x[:, None] * xx) % BRICK) / BRICK
        cos, sin = np.cos(angle), np.sin(angle)
        return np.block([[cos, sin], [-sin, cos]])

    t, j, k1x = (a.reshape(-1) for a in np.meshgrid(np.arange(4), np.arange(4), np.arange(8), indexing="ij"))
    main = block(4 * t + j, k1x)
    j, t = (a.reshape(-1) for a in np.meshgrid(np.arange(4), np.arange(8), indexing="ij"))
    last = block(4 * (t % 4) + j, np.full(32, 8))
    return halves_np(np.concatenate([main, last], axis=0))


def lap_tables():
    along_x = 4.0 * np.sin(np.pi * np.arange(288) / PLANE) ** 2
    along_y = 4.0 * np.sin(np.pi * np.arange(PLANE) / PLANE) ** 2
    rows = along_x[:256].reshape(8, 32).T
    lap_x = np.broadcast_to(rows[:, :, None], (32, 8, 128)).astype(np.float32)
    lap_y = np.broadcast_to(along_y.reshape(4, 1, 128), (4, 8, 128)).astype(np.float32)
    return lap_x, lap_y


def split(values):
    high = values.astype(BF16)
    return high, (values - high.astype(F32)).astype(BF16)


def dot(a, b):
    return jnp.dot(a, b, preferred_element_type=F32)


def dot3(a_high, a_low, b_high, b_low):
    return dot(a_high, b_high) + dot(a_high, b_low) + dot(a_low, b_high)


def send_kernel(bricks, xy, live, out):
    for h in range(2):
        for i in range(8):
            block = bricks[i * 128 : i * 128 + 128, h * 128 : h * 128 + 128]
            out[pl.ds(h * 128 * CHUNK + i, 128, stride=CHUNK), :] = block.T
    slot = lax.broadcasted_iota(jnp.int32, (1, SLOTS), 1)
    count = jnp.zeros((1, SLOTS), jnp.int32)
    for q in range(LAYERS):
        count = jnp.where(slot // CAP == q, live[0, q], count)
    place = jnp.where(slot % CAP < count, xy[0:1, :] * BLOCKS + xy[1:2, :], -1)
    place = jnp.concatenate([place, jnp.full((1, 128 - SLOTS), -1, jnp.int32)], axis=1)
    out[pl.ds(8, DEVICES, stride=CHUNK), :] = jnp.broadcast_to(place.astype(F32), (DEVICES, 128))


def send(bricks, xy, live):
    return pl.pallas_call(
        send_kernel,
        out_shape=jax.ShapeDtypeStruct((DEVICES * CHUNK, 128), F32),
        in_specs=[
            pl.BlockSpec(memory_space=pltpu.VMEM),
            pl.BlockSpec(memory_space=pltpu.VMEM),
            pl.BlockSpec(memory_space=pltpu.SMEM),
        ],
        out_specs=pl.BlockSpec(memory_space=pltpu.VMEM),
        compiler_params=pltpu.CompilerParams(vmem_limit_bytes=56 << 20),
        name="send",
    )(bricks, xy, live)


def read_cells(got, cells, places):
    for i in range(8):
        block = got[pl.ds(i, DEVICES, stride=CHUNK), :].T
        for h in range(2):
            at = h * 1024 + i * 128
            cells[at : at + 128, :] = block[:, h * 128 : h * 128 + 128]
    codes = got[pl.ds(8, DEVICES, stride=CHUNK), :]
    for q in range(LAYERS):
        places[q] = codes if q == 0 else pltpu.roll(codes, 128 - q * CAP, 1)


def spread_cells(cells, q, c, h, lane_group):
    tops, lows = [], []
    for parity in range(2):
        row = cells[pl.ds(h * 1024 + q * 256 + c * 16 + parity, 8, stride=2), :]
        tops.append(row.astype(BF16).astype(F32))
        lows.append(row - tops[-1])
    spread = [jnp.where(lane_group == g, piece, 0.0) for piece in tops + lows for g in range(4)]
    return jnp.concatenate(spread, axis=0).astype(BF16)


def place_layers(cells, places, field_high, field_low):
    lane_group = lax.broadcasted_iota(jnp.int32, (8, 128), 1) // 32
    site = lax.broadcasted_iota(jnp.int32, (128, SITES), 1).astype(F32)

    def place_layer(q, _):
        for h in range(2):
            where = places[q, h * 128 : h * 128 + 128, :]
            total = None
            for first in range(0, CAP, TOGETHER):
                slots = range(first, first + TOGETHER)
                spread = [spread_cells(cells, q, c, h, lane_group) for c in slots]
                chosen = [jnp.where(where[:, c : c + 1] == site, 1.0, 0.0).astype(BF16) for c in slots]
                part = dot(jnp.concatenate(spread, axis=1), jnp.concatenate(chosen, axis=0))
                total = part if total is None else total + part
            layer = total[:64] + total[64:]
            x = [layer[:, k * 256 : k * 256 + 256] for k in range(4)]
            even, odd = x[0] + x[2], x[1] + x[3]
            high, low = split(
                jnp.concatenate([even + odd, even - odd, x[0] - x[2], x[1] - x[3]], axis=1)
            )
            for parity in range(2):
                at = pl.multiple_of(parity * 256 + q * 64 + h * 32, 32)
                field_high[pl.ds(at, 32), :] = high[parity * 32 : parity * 32 + 32]
                field_low[pl.ds(at, 32), :] = low[parity * 32 : parity * 32 + 32]
        return 0

    lax.fori_loop(0, LAYERS, place_layer, 0, unroll=True)


def middle_kernel(
    got_any, twiddle, lat_any, dep_any, out_any,
    got, lat, dep, field_high, field_low, cells, places, out, sems,
):
    fetch_got = pltpu.make_async_copy(got_any, got, sems.at[0])
    fetch_got.start()
    fetch_dep = pltpu.make_async_copy(dep_any, dep, sems.at[1])
    fetch_dep.start()
    fetch_lat = [pltpu.make_async_copy(lat_any.at[k], lat.at[k], sems.at[2 + k]) for k in range(4)]
    for fetch in fetch_lat:
        fetch.start()
    fetch_got.wait()
    read_cells(got, cells, places)
    place_layers(cells, places, field_high, field_low)
    fetch_dep.wait()
    leave = []
    for k in range(4):
        fetch_lat[k].wait()
        cols = slice(512, 1024) if k % 2 else slice(k * 128, k * 128 + 256)
        used = slice(0, 512) if k % 2 else slice(0, 256)
        found = dot3(field_high[:, cols], field_low[:, cols], lat[k, 0, used, :], lat[k, 1, used, :])
        turn_re = twiddle[0:1, k * 256 : k * 256 + 256]
        turn_im = twiddle[1:2, k * 256 : k * 256 + 256]
        real = found[:, 0:256] * turn_re - found[:, 256:512] * turn_im
        imag = found[:, 0:256] * turn_im + found[:, 256:512] * turn_re
        sums = []
        for parity in range(2):
            rows = slice(parity * 256, parity * 256 + 256)
            high, low = split(jnp.concatenate([real[rows], imag[rows]], axis=0))
            sums.append(dot3(dep[0, parity], dep[1, parity], high, low))
        flat = out.at[k].reshape(DEVICES * 8, 128)
        for b in range(2):
            both = sums[0] + sums[1] if b == 0 else sums[0] - sums[1]
            for ri in range(2):
                for h in range(2):
                    flat[pl.ds((b * 2 + ri) * 2 + h, DEVICES, stride=8), :] = both[
                        ri * 256 : ri * 256 + 256, h * 128 : h * 128 + 128
                    ]
        leave.append(
            pltpu.make_async_copy(out.at[k], out_any.at[:, k * 8 : k * 8 + 8, :], sems.at[6 + k])
        )
        leave[k].start()
    for copy in leave:
        copy.wait()


def middle(got, twiddle):
    lat = jnp.asarray(np.stack(lattice_tables(), axis=1))
    dep = jnp.asarray(np.stack(depth_tables()))
    hbm = pl.BlockSpec(memory_space=pltpu.HBM)
    return pl.pallas_call(
        middle_kernel,
        out_shape=jax.ShapeDtypeStruct((DEVICES, 32, 128), F32),
        in_specs=[
            pl.BlockSpec(memory_space=pl.ANY),
            pl.BlockSpec(memory_space=pltpu.VMEM),
            hbm,
            hbm,
        ],
        out_specs=hbm,
        scratch_shapes=[
            pltpu.VMEM((DEVICES * CHUNK, 128), F32),
            pltpu.VMEM(lat.shape, BF16),
            pltpu.VMEM(dep.shape, BF16),
            pltpu.VMEM((NZ, SITES), BF16),
            pltpu.VMEM((NZ, SITES), BF16),
            pltpu.VMEM((2 * SLOTS * BRICK, 128), F32),
            pltpu.VMEM((LAYERS, DEVICES, 128), F32),
            pltpu.VMEM((4, DEVICES, 8, 128), F32),
            pltpu.SemaphoreType.DMA((10,)),
        ],
        compiler_params=pltpu.CompilerParams(vmem_limit_bytes=50 << 20),
        name="middle",
    )(got, twiddle, lat, dep)


def final_kernel(
    pieces_any, lap_z, lap_x, lap_y, cell_high, cell_low, out_re, out_im, pieces, sems
):
    block = lax.broadcasted_iota(jnp.int32, (8, 128), 1) // 32
    scale = -1.0 / math.sqrt(PLANE * PLANE * NZ)
    outs = (out_re, out_im)
    fetches = [
        pltpu.make_async_copy(pieces_any.at[:, k * 8 : k * 8 + 8, :], pieces.at[k], sems.at[k])
        for k in range(4)
    ]
    for fetch in fetches:
        fetch.start()
    for k in range(4):
        if k % FETCHED == 0:
            for fetch in fetches[k : k + FETCHED]:
                fetch.wait()
        flat = pieces.at[k].reshape(DEVICES * 8, 128)
        for b in range(2):
            parts = []
            for ri in range(2):
                halves = [flat[pl.ds((b * 2 + ri) * 2 + h, DEVICES, stride=8), :] for h in range(2)]
                parts.append(jnp.concatenate(halves, axis=1))
            high, low = split(jnp.concatenate(parts, axis=0))
            result = dot3(cell_high[0:256, :], cell_low[0:256, :], high, low)
            along_z = lap_z[b]
            for h in range(2):
                along_x = [lap_x[k + 16 * h + 4 * r] + (along_z + SCREEN) for r in range(4)]
                for t in range(4):
                    tiles = []
                    for ri in range(2):
                        at = ri * 128 + t * 32
                        row = [
                            result[at + j * 8 : at + j * 8 + 8, h * 128 : h * 128 + 128]
                            for j in range(4)
                        ]
                        tiles.append(transpose_blocks(row, block))
                    for r in range(4):
                        kx = k + 16 * h + 4 * r
                        factor = scale / (along_x[r] + lap_y[t])
                        for ri in range(2):
                            outs[ri][pl.ds(kx * 8 + t * 2 + b, 8, stride=256), :] = (
                                tiles[ri][r] * factor
                            )
            if k > 0:
                continue
            last = dot3(cell_high[256:320, :], cell_low[256:320, :], high[:, :128], low[:, :128])
            for ri in range(2):
                line = jnp.zeros((8, 128), F32)
                for j in range(4):
                    part = last[ri * 32 + j * 8 : ri * 32 + j * 8 + 8, :]
                    moved = part if j == 0 else pltpu.roll(part, 32 * j, 1)
                    line = jnp.where(block == j, moved, line)
                for t in range(4):
                    factor = scale / (along_z + 4.0 + lap_y[t, 0:1] + SCREEN)
                    outs[ri][2048 + t * 2 + b : 2049 + t * 2 + b, :] = line[t : t + 1] * factor


def transpose_blocks(row, block):
    low, even = block < 2, block % 2 == 0
    first = [jnp.where(low, row[j], pltpu.roll(row[j + 2], 64, 1)) for j in range(2)]
    last = [jnp.where(low, pltpu.roll(row[j], 64, 1), row[j + 2]) for j in range(2)]
    tiles = []
    for a, b in (first, last):
        tiles.append(jnp.where(even, a, pltpu.roll(b, 32, 1)))
        tiles.append(jnp.where(even, pltpu.roll(a, 96, 1), b))
    return tiles


def final(pieces, lap_z):
    lap_x, lap_y = lap_tables()
    tables = [jnp.asarray(t) for t in (lap_x, lap_y, *cell_tables())]
    shape = jax.ShapeDtypeStruct((KX * 8, 128), F32)
    vmem = pl.BlockSpec(memory_space=pltpu.VMEM)
    outs = pl.pallas_call(
        final_kernel,
        out_shape=(shape, shape),
        in_specs=[
            pl.BlockSpec(memory_space=pl.ANY),
            pl.BlockSpec(memory_space=pltpu.SMEM),
            *[vmem] * 4,
        ],
        out_specs=(vmem, vmem),
        scratch_shapes=[pltpu.VMEM((4, DEVICES, 8, 128), F32), pltpu.SemaphoreType.DMA((4,))],
        compiler_params=pltpu.CompilerParams(vmem_limit_bytes=24 << 20),
        name="final",
    )(pieces, lap_z, *tables)
    return tuple(
        o.reshape(KX, 4, 2, 128).transpose(2, 0, 1, 3).reshape(2, KX, PLANE) for o in outs
    )


def twiddle_of(device):
    yy = device // BRICK
    xx = device % BRICK
    column = jnp.arange(SITES, dtype=jnp.int32)
    kx = column // 256 + 4 * (column % 256 // BLOCKS)
    turn = (kx * xx + (column % BLOCKS) * yy) % PLANE
    angle = (2.0 * math.pi / PLANE) * turn.astype(F32)
    return jnp.stack([jnp.cos(angle), -jnp.sin(angle)])


def lap_z_of(device):
    kz = reverse_bits(2 * device + jnp.arange(2, dtype=jnp.int32), 9)
    return 4.0 * jnp.sin(math.pi * kz.astype(F32) / NZ) ** 2


def on_device(brick_data, brick_xy, brick_live):
    device = lax.axis_index("zg") * 32 + lax.axis_index("zl")
    sent = send(brick_data.reshape(SLOTS * BRICK, 256), brick_xy, brick_live.T)
    got = lax.all_to_all(sent.reshape(DEVICES, 1, CHUNK * 128), AXES, 0, 0, tiled=True)
    rows = middle(got.reshape(DEVICES * CHUNK, 128), twiddle_of(device))
    pieces = lax.all_to_all(rows, AXES, 0, 0, tiled=True)
    return final(pieces, lap_z_of(device))


def solution(mesh):
    in_specs = (P(AXES, None, None), P(None, AXES), P(None, AXES))
    out_specs = (P(AXES, None, None), P(AXES, None, None))
    return jax.shard_map(
        on_device, mesh=mesh, in_specs=in_specs, out_specs=out_specs, check_vma=False
    )
```

```python
import math

import jax
import jax.numpy as jnp
import numpy as np
from jax import lax
from jax.experimental import pallas as pl
from jax.experimental.pallas import tpu as pltpu
from jax.sharding import PartitionSpec as P

AXES = ("zg", "zl")
NZ = 512
PLANE = 512
BRICK = 16
BLOCKS = 32
LAYERS = 4
CAP = 16
GROUPS = 8
DEVICES = 256
KX = 257
SLOTS = LAYERS * CAP
SITES = BLOCKS * BLOCKS
SCREEN = 0.25
FETCHED = 2
TOGETHER = 4
CHUNK = 9
BF16 = jnp.bfloat16
F32 = jnp.float32


def reverse_bits(values, digits):
    result = values * 0
    for digit in range(digits):
        result = result | ((values >> digit) & 1) << (digits - 1 - digit)
    return result


def halves_np(table):
    high = table.astype(np.float32).astype(jnp.bfloat16)
    low = (table - high.astype(np.float64)).astype(np.float32).astype(jnp.bfloat16)
    return high, low


def lattice_tables():
    inner, by = np.divmod(np.arange(256), BLOCKS)
    k_high, ky = np.divmod(np.arange(256), BLOCKS)
    tables = []
    for k_low in range(4):
        turn = inner[:, None] * (k_low + 4 * k_high)[None, :] + by[:, None] * ky[None, :]
        angle = 2.0 * np.pi * (turn % BLOCKS) / BLOCKS
        real, imag = np.cos(angle), -np.sin(angle)
        if k_low == 1:
            below = [imag, -real]
        elif k_low == 3:
            below = [-imag, real]
        else:
            below = [0.0 * real, 0.0 * real]
        tables.append(np.block([[real, imag], below]))
    return halves_np(np.stack(tables))


def depth_tables():
    device = np.arange(DEVICES)
    kz_all = reverse_bits(2 * device, 9)
    q, g, zh = np.meshgrid(np.arange(LAYERS), np.arange(4), np.arange(8), indexing="ij")
    tables = []
    for parity in range(2):
        for half in range(2):
            kz = kz_all[half * 128 : half * 128 + 128]
            z = (g * 64 + q * 16 + 2 * zh + parity).reshape(-1)
            angle = 2.0 * np.pi * (kz[:, None] * z[None, :] % NZ) / NZ
            cos, sin = np.cos(angle), np.sin(angle)
            tables.append(np.block([[cos, sin], [-sin, cos]]))
    return halves_np(np.stack(tables))


def cell_tables():
    yy, xx = np.divmod(np.arange(128), BRICK)

    def block(k1y, k1x):
        angle = 2.0 * np.pi * ((k1y[:, None] * yy + k1x[:, None] * xx) % BRICK) / BRICK
        cos, sin = np.cos(angle), np.sin(angle)
        return np.block([[cos, sin], [-sin, cos]])

    tables = []
    for odd in range(2):
        t, j, k1x = (a.reshape(-1) for a in np.meshgrid(np.arange(4), np.arange(2), np.arange(8), indexing="ij"))
        main = block(4 * t + 2 * j + odd, k1x)
        j, t = (a.reshape(-1) for a in np.meshgrid(np.arange(2), np.arange(8), indexing="ij"))
        last = block(4 * (t % 4) + 2 * j + odd, np.full(16, 8))
        tables.append(np.concatenate([main, last], axis=0))
    return halves_np(np.stack(tables))


def lap_tables():
    along_x = 4.0 * np.sin(np.pi * np.arange(288) / PLANE) ** 2
    along_y = 4.0 * np.sin(np.pi * np.arange(PLANE) / PLANE) ** 2
    rows = along_x[:256].reshape(8, 32).T
    lap_x = np.broadcast_to(rows[:, :, None], (32, 8, 128)).astype(np.float32)
    lap_y = np.broadcast_to(along_y.reshape(4, 1, 128), (4, 8, 128)).astype(np.float32)
    return lap_x, lap_y


def split(values):
    high = values.astype(BF16)
    return high, (values - high.astype(F32)).astype(BF16)


def dot(a, b):
    return jnp.dot(a, b, preferred_element_type=F32)


def dot3(a_high, a_low, b_high, b_low):
    return dot(a_high, b_high) + dot(a_high, b_low) + dot(a_low, b_high)


def send_kernel(bricks, xy, live, out):
    for h in range(2):
        for i in range(8):
            block = bricks[i * 128 : i * 128 + 128, h * 128 : h * 128 + 128]
            out[pl.ds(h * 128 * CHUNK + i, 128, stride=CHUNK), :] = block.T
    slot = lax.broadcasted_iota(jnp.int32, (1, SLOTS), 1)
    count = jnp.zeros((1, SLOTS), jnp.int32)
    for q in range(LAYERS):
        count = jnp.where(slot // CAP == q, live[0, q], count)
    place = jnp.where(slot % CAP < count, xy[0:1, :] * BLOCKS + xy[1:2, :], -1)
    place = jnp.concatenate([place, jnp.full((1, 128 - SLOTS), -1, jnp.int32)], axis=1)
    out[pl.ds(8, DEVICES, stride=CHUNK), :] = jnp.broadcast_to(place.astype(F32), (DEVICES, 128))


def send(bricks, xy, live):
    return pl.pallas_call(
        send_kernel,
        out_shape=jax.ShapeDtypeStruct((DEVICES * CHUNK, 128), F32),
        in_specs=[
            pl.BlockSpec(memory_space=pltpu.VMEM),
            pl.BlockSpec(memory_space=pltpu.VMEM),
            pl.BlockSpec(memory_space=pltpu.SMEM),
        ],
        out_specs=pl.BlockSpec(memory_space=pltpu.VMEM),
        compiler_params=pltpu.CompilerParams(vmem_limit_bytes=56 << 20),
        name="send",
    )(bricks, xy, live)


def read_cells(got, cells, places):
    for i in range(8):
        block = got[pl.ds(i, DEVICES, stride=CHUNK), :].T
        for h in range(2):
            at = h * 1024 + i * 128
            cells[at : at + 128, :] = block[:, h * 128 : h * 128 + 128]
    codes = got[pl.ds(8, DEVICES, stride=CHUNK), :]
    for q in range(LAYERS):
        places[q] = codes if q == 0 else pltpu.roll(codes, 128 - q * CAP, 1)


def spread_cells(cells, q, c, h, lane_group):
    tops, lows = [], []
    for parity in range(2):
        row = cells[pl.ds(h * 1024 + q * 256 + c * 16 + parity, 8, stride=2), :]
        tops.append(row.astype(BF16).astype(F32))
        lows.append(row - tops[-1])
    spread = [jnp.where(lane_group == g, piece, 0.0) for piece in tops + lows for g in range(4)]
    return jnp.concatenate(spread, axis=0).astype(BF16)


def place_layers(cells, places, field_high, field_low):
    lane_group = lax.broadcasted_iota(jnp.int32, (8, 128), 1) // 32
    site = lax.broadcasted_iota(jnp.int32, (128, SITES), 1).astype(F32)

    def place_layer(q, _):
        layers = []
        for h in range(2):
            where = places[q, h * 128 : h * 128 + 128, :]
            total = None
            for first in range(0, CAP, TOGETHER):
                slots = range(first, first + TOGETHER)
                spread = [spread_cells(cells, q, c, h, lane_group) for c in slots]
                chosen = [jnp.where(where[:, c : c + 1] == site, 1.0, 0.0).astype(BF16) for c in slots]
                part = dot(jnp.concatenate(spread, axis=1), jnp.concatenate(chosen, axis=0))
                total = part if total is None else total + part
            layers.append(total[:64] + total[64:])
        for half, layer in enumerate((layers[0] + layers[1], layers[0] - layers[1])):
            x = [layer[:, k * 256 : k * 256 + 256] for k in range(4)]
            even, odd = x[0] + x[2], x[1] + x[3]
            high, low = split(
                jnp.concatenate([even + odd, even - odd, x[0] - x[2], x[1] - x[3]], axis=1)
            )
            for parity in range(2):
                at = pl.multiple_of(parity * 256 + half * 128 + q * 32, 32)
                field_high[pl.ds(at, 32), :] = high[parity * 32 : parity * 32 + 32]
                field_low[pl.ds(at, 32), :] = low[parity * 32 : parity * 32 + 32]
        return 0

    lax.fori_loop(0, LAYERS, place_layer, 0, unroll=True)


def middle_kernel(
    got_any, twiddle, lat_any, dep_any, out_any,
    got, lat, dep, field_high, field_low, cells, places, out, sems,
):
    fetch_got = pltpu.make_async_copy(got_any, got, sems.at[0])
    fetch_got.start()
    fetch_dep = pltpu.make_async_copy(dep_any, dep, sems.at[1])
    fetch_dep.start()
    fetch_lat = [pltpu.make_async_copy(lat_any.at[k], lat.at[k], sems.at[2 + k]) for k in range(4)]
    for fetch in fetch_lat:
        fetch.start()
    fetch_got.wait()
    read_cells(got, cells, places)
    place_layers(cells, places, field_high, field_low)
    fetch_dep.wait()
    leave = []
    for k in range(4):
        fetch_lat[k].wait()
        cols = slice(512, 1024) if k % 2 else slice(k * 128, k * 128 + 256)
        used = slice(0, 512) if k % 2 else slice(0, 256)
        found = dot3(field_high[:, cols], field_low[:, cols], lat[k, 0, used, :], lat[k, 1, used, :])
        turn_re = twiddle[0:1, k * 256 : k * 256 + 256]
        turn_im = twiddle[1:2, k * 256 : k * 256 + 256]
        real = found[:, 0:256] * turn_re - found[:, 256:512] * turn_im
        imag = found[:, 0:256] * turn_im + found[:, 256:512] * turn_re
        flat = out.at[k].reshape(DEVICES * 8, 128)
        for half in range(2):
            sums = []
            for parity in range(2):
                rows = slice(parity * 256 + half * 128, parity * 256 + half * 128 + 128)
                high, low = split(jnp.concatenate([real[rows], imag[rows]], axis=0))
                at = parity * 2 + half
                sums.append(dot3(dep[0, at], dep[1, at], high, low))
            for b in range(2):
                both = sums[0] + sums[1] if b == 0 else sums[0] - sums[1]
                for ri in range(2):
                    for h in range(2):
                        at = half * 128 * 8 + (b * 2 + ri) * 2 + h
                        flat[pl.ds(at, 128, stride=8), :] = both[
                            ri * 128 : ri * 128 + 128, h * 128 : h * 128 + 128
                        ]
        leave.append(
            pltpu.make_async_copy(out.at[k], out_any.at[:, k * 8 : k * 8 + 8, :], sems.at[6 + k])
        )
        leave[k].start()
    for copy in leave:
        copy.wait()


def middle(got, twiddle):
    lat = jnp.asarray(np.stack(lattice_tables(), axis=1))
    dep = jnp.asarray(np.stack(depth_tables()))
    hbm = pl.BlockSpec(memory_space=pltpu.HBM)
    return pl.pallas_call(
        middle_kernel,
        out_shape=jax.ShapeDtypeStruct((DEVICES, 32, 128), F32),
        in_specs=[
            pl.BlockSpec(memory_space=pl.ANY),
            pl.BlockSpec(memory_space=pltpu.VMEM),
            hbm,
            hbm,
        ],
        out_specs=hbm,
        scratch_shapes=[
            pltpu.VMEM((DEVICES * CHUNK, 128), F32),
            pltpu.VMEM(lat.shape, BF16),
            pltpu.VMEM(dep.shape, BF16),
            pltpu.VMEM((NZ, SITES), BF16),
            pltpu.VMEM((NZ, SITES), BF16),
            pltpu.VMEM((2 * SLOTS * BRICK, 128), F32),
            pltpu.VMEM((LAYERS, DEVICES, 128), F32),
            pltpu.VMEM((4, DEVICES, 8, 128), F32),
            pltpu.SemaphoreType.DMA((10,)),
        ],
        compiler_params=pltpu.CompilerParams(vmem_limit_bytes=50 << 20),
        name="middle",
    )(got, twiddle, lat, dep)


def final_kernel(
    pieces_any, lap_z, lap_x, lap_y, cell_high, cell_low, out_re, out_im, pieces, sems
):
    block = lax.broadcasted_iota(jnp.int32, (8, 128), 1) // 32
    scale = -1.0 / math.sqrt(PLANE * PLANE * NZ)
    outs = (out_re, out_im)
    fetches = [
        pltpu.make_async_copy(pieces_any.at[:, k * 8 : k * 8 + 8, :], pieces.at[k], sems.at[k])
        for k in range(4)
    ]
    for fetch in fetches:
        fetch.start()
    for k in range(4):
        if k % FETCHED == 0:
            for fetch in fetches[k : k + FETCHED]:
                fetch.wait()
        flat = pieces.at[k].reshape(DEVICES * 8, 128)
        for b in range(2):
            sides = []
            for side in range(2):
                parts = []
                for ri in range(2):
                    at = side * 128 * 8 + (b * 2 + ri) * 2
                    parts.append([flat[pl.ds(at + h, 128, stride=8), :] for h in range(2)])
                sides.append(jnp.concatenate([jnp.concatenate(p, axis=1) for p in parts], axis=0))
            folded = [split(sides[0] + sides[1]), split(sides[0] - sides[1])]
            results = [
                dot3(cell_high[odd, 0:128, :], cell_low[odd, 0:128, :], *folded[odd])
                for odd in range(2)
            ]
            along_z = lap_z[b]
            for h in range(2):
                along_x = [lap_x[k + 16 * h + 4 * r] + (along_z + SCREEN) for r in range(4)]
                for t in range(4):
                    tiles = []
                    for ri in range(2):
                        at = ri * 64 + t * 16
                        row = [
                            results[j % 2][
                                at + j // 2 * 8 : at + j // 2 * 8 + 8, h * 128 : h * 128 + 128
                            ]
                            for j in range(4)
                        ]
                        tiles.append(transpose_blocks(row, block))
                    for r in range(4):
                        kx = k + 16 * h + 4 * r
                        factor = scale / (along_x[r] + lap_y[t])
                        for ri in range(2):
                            outs[ri][pl.ds(kx * 8 + t * 2 + b, 8, stride=256), :] = (
                                tiles[ri][r] * factor
                            )
            if k > 0:
                continue
            lasts = [
                dot3(
                    cell_high[odd, 128:160, :], cell_low[odd, 128:160, :], folded[odd][0][:, :128], folded[odd][1][:, :128]
                )
                for odd in range(2)
            ]
            for ri in range(2):
                line = jnp.zeros((8, 128), F32)
                for j in range(4):
                    at = ri * 16 + j // 2 * 8
                    part = lasts[j % 2][at : at + 8, :]
                    moved = part if j == 0 else pltpu.roll(part, 32 * j, 1)
                    line = jnp.where(block == j, moved, line)
                for t in range(4):
                    factor = scale / (along_z + 4.0 + lap_y[t, 0:1] + SCREEN)
                    outs[ri][2048 + t * 2 + b : 2049 + t * 2 + b, :] = line[t : t + 1] * factor


def transpose_blocks(row, block):
    low, even = block < 2, block % 2 == 0
    first = [jnp.where(low, row[j], pltpu.roll(row[j + 2], 64, 1)) for j in range(2)]
    last = [jnp.where(low, pltpu.roll(row[j], 64, 1), row[j + 2]) for j in range(2)]
    tiles = []
    for a, b in (first, last):
        tiles.append(jnp.where(even, a, pltpu.roll(b, 32, 1)))
        tiles.append(jnp.where(even, pltpu.roll(a, 96, 1), b))
    return tiles


def final(pieces, lap_z):
    lap_x, lap_y = lap_tables()
    tables = [jnp.asarray(t) for t in (lap_x, lap_y, *cell_tables())]
    shape = jax.ShapeDtypeStruct((KX * 8, 128), F32)
    vmem = pl.BlockSpec(memory_space=pltpu.VMEM)
    outs = pl.pallas_call(
        final_kernel,
        out_shape=(shape, shape),
        in_specs=[
            pl.BlockSpec(memory_space=pl.ANY),
            pl.BlockSpec(memory_space=pltpu.SMEM),
            *[vmem] * 4,
        ],
        out_specs=(vmem, vmem),
        scratch_shapes=[pltpu.VMEM((4, DEVICES, 8, 128), F32), pltpu.SemaphoreType.DMA((4,))],
        compiler_params=pltpu.CompilerParams(vmem_limit_bytes=24 << 20),
        name="final",
    )(pieces, lap_z, *tables)
    return tuple(
        o.reshape(KX, 4, 2, 128).transpose(2, 0, 1, 3).reshape(2, KX, PLANE) for o in outs
    )


def twiddle_of(device):
    yy = device // BRICK
    xx = device % BRICK
    column = jnp.arange(SITES, dtype=jnp.int32)
    kx = column // 256 + 4 * (column % 256 // BLOCKS)
    turn = (kx * xx + (column % BLOCKS) * yy) % PLANE
    angle = (2.0 * math.pi / PLANE) * turn.astype(F32)
    return jnp.stack([jnp.cos(angle), -jnp.sin(angle)])


def lap_z_of(device):
    kz = reverse_bits(2 * device + jnp.arange(2, dtype=jnp.int32), 9)
    return 4.0 * jnp.sin(math.pi * kz.astype(F32) / NZ) ** 2


def on_device(brick_data, brick_xy, brick_live):
    device = lax.axis_index("zg") * 32 + lax.axis_index("zl")
    sent = send(brick_data.reshape(SLOTS * BRICK, 256), brick_xy, brick_live.T)
    got = lax.all_to_all(sent.reshape(DEVICES, 1, CHUNK * 128), AXES, 0, 0, tiled=True)
    rows = middle(got.reshape(DEVICES * CHUNK, 128), twiddle_of(device))
    pieces = lax.all_to_all(rows, AXES, 0, 0, tiled=True)
    return final(pieces, lap_z_of(device))


def solution(mesh):
    in_specs = (P(AXES, None, None), P(None, AXES), P(None, AXES))
    out_specs = (P(AXES, None, None), P(AXES, None, None))
    return jax.shard_map(
        on_device, mesh=mesh, in_specs=in_specs, out_specs=out_specs, check_vma=False
    )
```

```python
import math

import jax
import jax.numpy as jnp
import numpy as np
from jax import lax
from jax.experimental import pallas as pl
from jax.experimental.pallas import tpu as pltpu
from jax.sharding import PartitionSpec as P

AXES = ("zg", "zl")
NZ = 512
PLANE = 512
BRICK = 16
BLOCKS = 32
LAYERS = 4
CAP = 16
GROUPS = 8
DEVICES = 256
KX = 257
SLOTS = LAYERS * CAP
SITES = BLOCKS * BLOCKS
SCREEN = 0.25
FETCHED = 2
TOGETHER = 4
CHUNK = 9
BF16 = jnp.bfloat16
F32 = jnp.float32


def reverse_bits(values, digits):
    result = values * 0
    for digit in range(digits):
        result = result | ((values >> digit) & 1) << (digits - 1 - digit)
    return result


def halves_np(table):
    high = table.astype(np.float32).astype(jnp.bfloat16)
    low = (table - high.astype(np.float64)).astype(np.float32).astype(jnp.bfloat16)
    return high, low


def lattice_tables():
    inner, by = np.divmod(np.arange(256), BLOCKS)
    k_high, ky = np.divmod(np.arange(256), BLOCKS)
    tables = []
    for k_low in range(4):
        turn = inner[:, None] * (k_low + 4 * k_high)[None, :] + by[:, None] * ky[None, :]
        angle = 2.0 * np.pi * (turn % BLOCKS) / BLOCKS
        real, imag = np.cos(angle), -np.sin(angle)
        if k_low == 1:
            below = [imag, -real]
        elif k_low == 3:
            below = [-imag, real]
        else:
            below = [0.0 * real, 0.0 * real]
        tables.append(np.block([[real, imag], below]))
    return halves_np(np.stack(tables))


def depth_tables():
    device = np.arange(DEVICES)
    kz_all = reverse_bits(2 * device, 9)
    q, g, zh = np.meshgrid(np.arange(LAYERS), np.arange(4), np.arange(8), indexing="ij")
    tables = []
    for parity in range(2):
        for half in range(2):
            kz = kz_all[half * 128 : half * 128 + 128]
            z = (g * 64 + q * 16 + 2 * zh + parity).reshape(-1)
            angle = 2.0 * np.pi * (kz[:, None] * z[None, :] % NZ) / NZ
            cos, sin = np.cos(angle), np.sin(angle)
            tables.append(np.block([[cos, sin], [-sin, cos]]))
    return halves_np(np.stack(tables))


def cell_tables():
    yy, xx = np.divmod(np.arange(128), BRICK)

    def block(k1y, k1x):
        angle = 2.0 * np.pi * ((k1y[:, None] * yy + k1x[:, None] * xx) % BRICK) / BRICK
        cos, sin = np.cos(angle), np.sin(angle)
        return np.block([[cos, sin], [-sin, cos]])

    tables = []
    for odd in range(2):
        t, j, k1x = (a.reshape(-1) for a in np.meshgrid(np.arange(4), np.arange(2), np.arange(8), indexing="ij"))
        main = block(4 * t + 2 * j + odd, k1x)
        j, t = (a.reshape(-1) for a in np.meshgrid(np.arange(2), np.arange(8), indexing="ij"))
        last = block(4 * (t % 4) + 2 * j + odd, np.full(16, 8))
        tables.append(np.concatenate([main, last], axis=0))
    return halves_np(np.stack(tables))


def lap_tables():
    along_x = 4.0 * np.sin(np.pi * np.arange(288) / PLANE) ** 2
    along_y = 4.0 * np.sin(np.pi * np.arange(PLANE) / PLANE) ** 2
    rows = along_x[:256].reshape(8, 32).T
    lap_x = np.broadcast_to(rows[:, :, None], (32, 8, 128)).astype(np.float32)
    lap_y = np.broadcast_to(along_y.reshape(4, 1, 128), (4, 8, 128)).astype(np.float32)
    return lap_x, lap_y


def split(values):
    high = values.astype(BF16)
    return high, (values - high.astype(F32)).astype(BF16)


def dot(a, b):
    return jnp.dot(a, b, preferred_element_type=F32)


def dot3(a_high, a_low, b_high, b_low):
    return dot(a_high, b_high) + dot(a_high, b_low) + dot(a_low, b_high)


def send_kernel(bricks, xy, live, out):
    for h in range(2):
        for i in range(8):
            block = bricks[i * 128 : i * 128 + 128, h * 128 : h * 128 + 128]
            out[pl.ds(h * 128 * CHUNK + i, 128, stride=CHUNK), :] = block.T
    slot = lax.broadcasted_iota(jnp.int32, (1, SLOTS), 1)
    count = jnp.zeros((1, SLOTS), jnp.int32)
    for q in range(LAYERS):
        count = jnp.where(slot // CAP == q, live[0, q], count)
    place = jnp.where(slot % CAP < count, xy[0:1, :] * BLOCKS + xy[1:2, :], -1)
    place = jnp.concatenate([place, jnp.full((1, 128 - SLOTS), -1, jnp.int32)], axis=1)
    out[pl.ds(8, DEVICES, stride=CHUNK), :] = jnp.broadcast_to(place.astype(F32), (DEVICES, 128))


def send(bricks, xy, live):
    return pl.pallas_call(
        send_kernel,
        out_shape=jax.ShapeDtypeStruct((DEVICES * CHUNK, 128), F32),
        in_specs=[
            pl.BlockSpec(memory_space=pltpu.VMEM),
            pl.BlockSpec(memory_space=pltpu.VMEM),
            pl.BlockSpec(memory_space=pltpu.SMEM),
        ],
        out_specs=pl.BlockSpec(memory_space=pltpu.VMEM),
        compiler_params=pltpu.CompilerParams(vmem_limit_bytes=56 << 20),
        name="send",
    )(bricks, xy, live)


def read_cells(got, cells, places):
    for i in range(8):
        block = got[pl.ds(i, DEVICES, stride=CHUNK), :].T
        for h in range(2):
            at = h * 1024 + i * 128
            cells[at : at + 128, :] = block[:, h * 128 : h * 128 + 128]
    codes = got[pl.ds(8, DEVICES, stride=CHUNK), :]
    for q in range(LAYERS):
        places[q] = codes if q == 0 else pltpu.roll(codes, 128 - q * CAP, 1)


def spread_cells(cells, q, c, h, lane_group):
    tops, lows = [], []
    for parity in range(2):
        row = cells[pl.ds(h * 1024 + q * 256 + c * 16 + parity, 8, stride=2), :]
        tops.append(row.astype(BF16).astype(F32))
        lows.append(row - tops[-1])
    spread = [jnp.where(lane_group == g, piece, 0.0) for piece in tops + lows for g in range(4)]
    return jnp.concatenate(spread, axis=0).astype(BF16)


def place_layers(cells, places, field_high, field_low):
    lane_group = lax.broadcasted_iota(jnp.int32, (8, 128), 1) // 32
    site = lax.broadcasted_iota(jnp.int32, (128, SITES), 1).astype(F32)

    def place_layer(q, _):
        layers = []
        for h in range(2):
            where = places[q, h * 128 : h * 128 + 128, :]
            total = None
            for first in range(0, CAP, TOGETHER):
                slots = range(first, first + TOGETHER)
                spread = [spread_cells(cells, q, c, h, lane_group) for c in slots]
                chosen = [jnp.where(where[:, c : c + 1] == site, 1.0, 0.0).astype(BF16) for c in slots]
                part = dot(jnp.concatenate(spread, axis=1), jnp.concatenate(chosen, axis=0))
                total = part if total is None else total + part
            layers.append(total[:64] + total[64:])
        for half, layer in enumerate((layers[0] + layers[1], layers[0] - layers[1])):
            x = [layer[:, k * 256 : k * 256 + 256] for k in range(4)]
            even, odd = x[0] + x[2], x[1] + x[3]
            high, low = split(
                jnp.concatenate([even + odd, even - odd, x[0] - x[2], x[1] - x[3]], axis=1)
            )
            for parity in range(2):
                at = pl.multiple_of(parity * 256 + half * 128 + q * 32, 32)
                field_high[pl.ds(at, 32), :] = high[parity * 32 : parity * 32 + 32]
                field_low[pl.ds(at, 32), :] = low[parity * 32 : parity * 32 + 32]
        return 0

    lax.fori_loop(0, LAYERS, place_layer, 0, unroll=True)


def middle_kernel(
    got_any, twiddle, lat_any, dep_any, out_any,
    got, lat, dep, field_high, field_low, cells, places, out, sems,
):
    fetch_got = pltpu.make_async_copy(got_any, got, sems.at[0])
    fetch_got.start()
    fetch_dep = pltpu.make_async_copy(dep_any, dep, sems.at[1])
    fetch_dep.start()
    fetch_lat = [pltpu.make_async_copy(lat_any.at[k], lat.at[k], sems.at[2 + k]) for k in range(4)]
    for fetch in fetch_lat:
        fetch.start()
    fetch_got.wait()
    read_cells(got, cells, places)
    place_layers(cells, places, field_high, field_low)
    for fetch in (fetch_dep, *fetch_lat):
        fetch.wait()
    leave = []

    def lattice(k):
        cols = slice(512, 1024) if k % 2 else slice(k * 128, k * 128 + 256)
        used = slice(0, 512) if k % 2 else slice(0, 256)
        return dot3(field_high[:, cols], field_low[:, cols], lat[k, 0, used, :], lat[k, 1, used, :])

    ahead = lattice(0)
    for k in range(4):
        found = ahead
        if k < 3:
            ahead = lattice(k + 1)
        turn_re = twiddle[0:1, k * 256 : k * 256 + 256]
        turn_im = twiddle[1:2, k * 256 : k * 256 + 256]
        real = found[:, 0:256] * turn_re - found[:, 256:512] * turn_im
        imag = found[:, 0:256] * turn_im + found[:, 256:512] * turn_re
        flat = out.at[k].reshape(DEVICES * 8, 128)
        for half in range(2):
            sums = []
            for parity in range(2):
                rows = slice(parity * 256 + half * 128, parity * 256 + half * 128 + 128)
                high, low = split(jnp.concatenate([real[rows], imag[rows]], axis=0))
                at = parity * 2 + half
                sums.append(dot3(dep[0, at], dep[1, at], high, low))
            for b in range(2):
                both = sums[0] + sums[1] if b == 0 else sums[0] - sums[1]
                for ri in range(2):
                    for h in range(2):
                        at = half * 128 * 8 + (b * 2 + ri) * 2 + h
                        flat[pl.ds(at, 128, stride=8), :] = both[
                            ri * 128 : ri * 128 + 128, h * 128 : h * 128 + 128
                        ]
        leave.append(
            pltpu.make_async_copy(out.at[k], out_any.at[:, k * 8 : k * 8 + 8, :], sems.at[6 + k])
        )
        leave[k].start()
    for copy in leave:
        copy.wait()


def middle(got, twiddle):
    lat = jnp.asarray(np.stack(lattice_tables(), axis=1))
    dep = jnp.asarray(np.stack(depth_tables()))
    hbm = pl.BlockSpec(memory_space=pltpu.HBM)
    return pl.pallas_call(
        middle_kernel,
        out_shape=jax.ShapeDtypeStruct((DEVICES, 32, 128), F32),
        in_specs=[
            pl.BlockSpec(memory_space=pl.ANY),
            pl.BlockSpec(memory_space=pltpu.VMEM),
            hbm,
            hbm,
        ],
        out_specs=hbm,
        scratch_shapes=[
            pltpu.VMEM((DEVICES * CHUNK, 128), F32),
            pltpu.VMEM(lat.shape, BF16),
            pltpu.VMEM(dep.shape, BF16),
            pltpu.VMEM((NZ, SITES), BF16),
            pltpu.VMEM((NZ, SITES), BF16),
            pltpu.VMEM((2 * SLOTS * BRICK, 128), F32),
            pltpu.VMEM((LAYERS, DEVICES, 128), F32),
            pltpu.VMEM((4, DEVICES, 8, 128), F32),
            pltpu.SemaphoreType.DMA((10,)),
        ],
        compiler_params=pltpu.CompilerParams(vmem_limit_bytes=50 << 20),
        name="middle",
    )(got, twiddle, lat, dep)


def final_kernel(
    pieces_any, lap_z, lap_x, lap_y, cell_high, cell_low, out_re, out_im, pieces, sems
):
    block = lax.broadcasted_iota(jnp.int32, (8, 128), 1) // 32
    scale = -1.0 / math.sqrt(PLANE * PLANE * NZ)
    outs = (out_re, out_im)
    fetches = [
        pltpu.make_async_copy(pieces_any.at[:, k * 8 : k * 8 + 8, :], pieces.at[k], sems.at[k])
        for k in range(4)
    ]
    for fetch in fetches:
        fetch.start()
    for k in range(4):
        if k % FETCHED == 0:
            for fetch in fetches[k : k + FETCHED]:
                fetch.wait()
        flat = pieces.at[k].reshape(DEVICES * 8, 128)
        for b in range(2):
            sides = []
            for side in range(2):
                parts = []
                for ri in range(2):
                    at = side * 128 * 8 + (b * 2 + ri) * 2
                    parts.append([flat[pl.ds(at + h, 128, stride=8), :] for h in range(2)])
                sides.append(jnp.concatenate([jnp.concatenate(p, axis=1) for p in parts], axis=0))
            folded = [split(sides[0] + sides[1]), split(sides[0] - sides[1])]
            results = [
                dot3(cell_high[odd, 0:128, :], cell_low[odd, 0:128, :], *folded[odd])
                for odd in range(2)
            ]
            along_z = lap_z[b]
            for h in range(2):
                along_x = [lap_x[k + 16 * h + 4 * r] + (along_z + SCREEN) for r in range(4)]
                for t in range(4):
                    tiles = []
                    for ri in range(2):
                        at = ri * 64 + t * 16
                        row = [
                            results[j % 2][
                                at + j // 2 * 8 : at + j // 2 * 8 + 8, h * 128 : h * 128 + 128
                            ]
                            for j in range(4)
                        ]
                        tiles.append(transpose_blocks(row, block))
                    for r in range(4):
                        kx = k + 16 * h + 4 * r
                        factor = scale / (along_x[r] + lap_y[t])
                        for ri in range(2):
                            outs[ri][pl.ds(kx * 8 + t * 2 + b, 8, stride=256), :] = (
                                tiles[ri][r] * factor
                            )
            if k > 0:
                continue
            lasts = [
                dot3(
                    cell_high[odd, 128:160, :], cell_low[odd, 128:160, :], folded[odd][0][:, :128], folded[odd][1][:, :128]
                )
                for odd in range(2)
            ]
            for ri in range(2):
                line = jnp.zeros((8, 128), F32)
                for j in range(4):
                    at = ri * 16 + j // 2 * 8
                    part = lasts[j % 2][at : at + 8, :]
                    moved = part if j == 0 else pltpu.roll(part, 32 * j, 1)
                    line = jnp.where(block == j, moved, line)
                for t in range(4):
                    factor = scale / (along_z + 4.0 + lap_y[t, 0:1] + SCREEN)
                    outs[ri][2048 + t * 2 + b : 2049 + t * 2 + b, :] = line[t : t + 1] * factor


def transpose_blocks(row, block):
    low, even = block < 2, block % 2 == 0
    first = [jnp.where(low, row[j], pltpu.roll(row[j + 2], 64, 1)) for j in range(2)]
    last = [jnp.where(low, pltpu.roll(row[j], 64, 1), row[j + 2]) for j in range(2)]
    tiles = []
    for a, b in (first, last):
        tiles.append(jnp.where(even, a, pltpu.roll(b, 32, 1)))
        tiles.append(jnp.where(even, pltpu.roll(a, 96, 1), b))
    return tiles


def final(pieces, lap_z):
    lap_x, lap_y = lap_tables()
    tables = [jnp.asarray(t) for t in (lap_x, lap_y, *cell_tables())]
    shape = jax.ShapeDtypeStruct((KX * 8, 128), F32)
    vmem = pl.BlockSpec(memory_space=pltpu.VMEM)
    outs = pl.pallas_call(
        final_kernel,
        out_shape=(shape, shape),
        in_specs=[
            pl.BlockSpec(memory_space=pl.ANY),
            pl.BlockSpec(memory_space=pltpu.SMEM),
            *[vmem] * 4,
        ],
        out_specs=(vmem, vmem),
        scratch_shapes=[pltpu.VMEM((4, DEVICES, 8, 128), F32), pltpu.SemaphoreType.DMA((4,))],
        compiler_params=pltpu.CompilerParams(vmem_limit_bytes=24 << 20),
        name="final",
    )(pieces, lap_z, *tables)
    return tuple(
        o.reshape(KX, 4, 2, 128).transpose(2, 0, 1, 3).reshape(2, KX, PLANE) for o in outs
    )


def twiddle_of(device):
    yy = device // BRICK
    xx = device % BRICK
    column = jnp.arange(SITES, dtype=jnp.int32)
    kx = column // 256 + 4 * (column % 256 // BLOCKS)
    turn = (kx * xx + (column % BLOCKS) * yy) % PLANE
    angle = (2.0 * math.pi / PLANE) * turn.astype(F32)
    return jnp.stack([jnp.cos(angle), -jnp.sin(angle)])


def lap_z_of(device):
    kz = reverse_bits(2 * device + jnp.arange(2, dtype=jnp.int32), 9)
    return 4.0 * jnp.sin(math.pi * kz.astype(F32) / NZ) ** 2


def on_device(brick_data, brick_xy, brick_live):
    device = lax.axis_index("zg") * 32 + lax.axis_index("zl")
    sent = send(brick_data.reshape(SLOTS * BRICK, 256), brick_xy, brick_live.T)
    got = lax.all_to_all(sent.reshape(DEVICES, 1, CHUNK * 128), AXES, 0, 0, tiled=True)
    rows = middle(got.reshape(DEVICES * CHUNK, 128), twiddle_of(device))
    pieces = lax.all_to_all(rows, AXES, 0, 0, tiled=True)
    return final(pieces, lap_z_of(device))


def solution(mesh):
    in_specs = (P(AXES, None, None), P(None, AXES), P(None, AXES))
    out_specs = (P(AXES, None, None), P(AXES, None, None))
    return jax.shard_map(
        on_device, mesh=mesh, in_specs=in_specs, out_specs=out_specs, check_vma=False
    )
```

```python
import math

import jax
import jax.numpy as jnp
import numpy as np
from jax import lax
from jax.experimental import pallas as pl
from jax.experimental.pallas import tpu as pltpu
from jax.sharding import PartitionSpec as P

AXES = ("zg", "zl")
NZ = 512
PLANE = 512
BRICK = 16
BLOCKS = 32
LAYERS = 4
CAP = 16
GROUPS = 8
DEVICES = 256
KX = 257
SLOTS = LAYERS * CAP
SITES = BLOCKS * BLOCKS
SCREEN = 0.25
PITCH = 264
TOGETHER = 4
CHUNK = 9
BF16 = jnp.bfloat16
F32 = jnp.float32


def reverse_bits(values, digits):
    result = values * 0
    for digit in range(digits):
        result = result | ((values >> digit) & 1) << (digits - 1 - digit)
    return result


def halves_np(table):
    high = table.astype(np.float32).astype(jnp.bfloat16)
    low = (table - high.astype(np.float64)).astype(np.float32).astype(jnp.bfloat16)
    return high, low


def lattice_tables():
    inner, by = np.divmod(np.arange(256), BLOCKS)
    k_high, ky = np.divmod(np.arange(256), BLOCKS)
    tables = []
    for k_low in range(4):
        turn = inner[:, None] * (k_low + 4 * k_high)[None, :] + by[:, None] * ky[None, :]
        angle = 2.0 * np.pi * (turn % BLOCKS) / BLOCKS
        real, imag = np.cos(angle), -np.sin(angle)
        if k_low == 1:
            below = [imag, -real]
        elif k_low == 3:
            below = [-imag, real]
        else:
            below = [0.0 * real, 0.0 * real]
        tables.append(np.block([[real, imag], below]))
    return halves_np(np.stack(tables))


def depth_tables():
    device = np.arange(DEVICES)
    kz_all = reverse_bits(2 * device, 9)
    q, g, zh = np.meshgrid(np.arange(LAYERS), np.arange(4), np.arange(8), indexing="ij")
    tables = []
    for parity in range(2):
        for half in range(2):
            kz = kz_all[half * 128 : half * 128 + 128]
            z = (g * 64 + q * 16 + 2 * zh + parity).reshape(-1)
            angle = 2.0 * np.pi * (kz[:, None] * z[None, :] % NZ) / NZ
            cos, sin = np.cos(angle), np.sin(angle)
            tables.append(np.block([[cos, sin], [-sin, cos]]))
    return halves_np(np.stack(tables))


def cell_tables():
    yy, xx = np.divmod(np.arange(128), BRICK)

    def block(k1y, k1x):
        angle = 2.0 * np.pi * ((k1y[:, None] * yy + k1x[:, None] * xx) % BRICK) / BRICK
        cos, sin = np.cos(angle), np.sin(angle)
        return np.block([[cos, sin], [-sin, cos]])

    tables = []
    for odd in range(2):
        t, j, k1x = (a.reshape(-1) for a in np.meshgrid(np.arange(4), np.arange(2), np.arange(8), indexing="ij"))
        main = block(4 * t + 2 * j + odd, k1x)
        j, t = (a.reshape(-1) for a in np.meshgrid(np.arange(2), np.arange(8), indexing="ij"))
        last = block(4 * (t % 4) + 2 * j + odd, np.full(16, 8))
        tables.append(np.concatenate([main, last], axis=0))
    return halves_np(np.stack(tables))


def lap_tables():
    along_x = 4.0 * np.sin(np.pi * np.arange(288) / PLANE) ** 2
    along_y = 4.0 * np.sin(np.pi * np.arange(PLANE) / PLANE) ** 2
    rows = along_x[:256].reshape(8, 32).T
    lap_x = np.broadcast_to(rows[:, :, None], (32, 8, 128)).astype(np.float32)
    lap_y = np.broadcast_to(along_y.reshape(4, 1, 128), (4, 8, 128)).astype(np.float32)
    return lap_x, lap_y


def split(values):
    high = values.astype(BF16)
    return high, (values - high.astype(F32)).astype(BF16)


def dot(a, b):
    return jnp.dot(a, b, preferred_element_type=F32)


def dot3(a_high, a_low, b_high, b_low):
    return dot(a_high, b_high) + dot(a_high, b_low) + dot(a_low, b_high)


def send_kernel(bricks, xy, live, out):
    for i in range(8):
        out[pl.ds(i, 128, stride=CHUNK), :] = bricks[i * 128 : i * 128 + 128, :].T
    slot = lax.broadcasted_iota(jnp.int32, (1, SLOTS), 1)
    count = jnp.zeros((1, SLOTS), jnp.int32)
    for q in range(LAYERS):
        count = jnp.where(slot // CAP == q, live[0, q], count)
    place = jnp.where(slot % CAP < count, xy[0:1, :] * BLOCKS + xy[1:2, :], -1)
    place = jnp.concatenate([place, jnp.full((1, 128 - SLOTS), -1, jnp.int32)], axis=1)
    out[pl.ds(8, 128, stride=CHUNK), :] = jnp.broadcast_to(place.astype(F32), (128, 128))


def send(bricks, xy, live):
    return pl.pallas_call(
        send_kernel,
        grid=(2,),
        out_shape=jax.ShapeDtypeStruct((DEVICES * CHUNK, 128), F32),
        in_specs=[
            pl.BlockSpec((SLOTS * BRICK, 128), lambda h: (0, h)),
            pl.BlockSpec(memory_space=pltpu.VMEM),
            pl.BlockSpec(memory_space=pltpu.SMEM),
        ],
        out_specs=pl.BlockSpec((128 * CHUNK, 128), lambda h: (h, 0)),
        compiler_params=pltpu.CompilerParams(vmem_limit_bytes=56 << 20),
        name="send",
    )(bricks, xy, live)


def read_cells(got, cells, places):
    for i in range(8):
        block = got[pl.ds(i, DEVICES, stride=CHUNK), :].T
        for h in range(2):
            at = h * 1024 + i * 128
            cells[at : at + 128, :] = block[:, h * 128 : h * 128 + 128]
    codes = got[pl.ds(8, DEVICES, stride=CHUNK), :]
    for q in range(LAYERS):
        places[q] = codes if q == 0 else pltpu.roll(codes, 128 - q * CAP, 1)


def spread_cells(cells, q, c, h, lane_group):
    tops, lows = [], []
    for parity in range(2):
        row = cells[pl.ds(h * 1024 + q * 256 + c * 16 + parity, 8, stride=2), :]
        tops.append(row.astype(BF16).astype(F32))
        lows.append(row - tops[-1])
    spread = [jnp.where(lane_group == g, piece, 0.0) for piece in tops + lows for g in range(4)]
    return jnp.concatenate(spread, axis=0).astype(BF16)


def place_layers(cells, places, field_high, field_low):
    lane_group = lax.broadcasted_iota(jnp.int32, (8, 128), 1) // 32
    site = lax.broadcasted_iota(jnp.int32, (128, SITES), 1).astype(F32)

    def place_layer(q, _):
        layers = []
        for h in range(2):
            where = places[q, h * 128 : h * 128 + 128, :]
            total = None
            for first in range(0, CAP, TOGETHER):
                slots = range(first, first + TOGETHER)
                spread = [spread_cells(cells, q, c, h, lane_group) for c in slots]
                chosen = [jnp.where(where[:, c : c + 1] == site, 1.0, 0.0).astype(BF16) for c in slots]
                part = dot(jnp.concatenate(spread, axis=1), jnp.concatenate(chosen, axis=0))
                total = part if total is None else total + part
            layers.append(total[:64] + total[64:])
        for half, layer in enumerate((layers[0] + layers[1], layers[0] - layers[1])):
            x = [layer[:, k * 256 : k * 256 + 256] for k in range(4)]
            even, odd = x[0] + x[2], x[1] + x[3]
            high, low = split(
                jnp.concatenate([even + odd, even - odd, x[0] - x[2], x[1] - x[3]], axis=1)
            )
            for parity in range(2):
                at = pl.multiple_of(parity * 256 + half * 128 + q * 32, 32)
                field_high[pl.ds(at, 32), :] = high[parity * 32 : parity * 32 + 32]
                field_low[pl.ds(at, 32), :] = low[parity * 32 : parity * 32 + 32]
        return 0

    lax.fori_loop(0, LAYERS, place_layer, 0, unroll=True)


def middle_kernel(
    got_any, twiddle, lat_any, dep_any, out_any,
    got, lat, dep, field_high, field_low, cells, places, out, sems,
):
    fetch_got = pltpu.make_async_copy(got_any, got, sems.at[0])
    fetch_got.start()
    fetch_dep = pltpu.make_async_copy(dep_any, dep, sems.at[1])
    fetch_dep.start()
    fetch_lat = [pltpu.make_async_copy(lat_any.at[k], lat.at[k], sems.at[2 + k]) for k in range(4)]
    for fetch in fetch_lat:
        fetch.start()
    fetch_got.wait()
    read_cells(got, cells, places)
    place_layers(cells, places, field_high, field_low)
    for fetch in (fetch_dep, *fetch_lat):
        fetch.wait()
    leave = []

    def lattice(k):
        cols = slice(512, 1024) if k % 2 else slice(k * 128, k * 128 + 256)
        used = slice(0, 512) if k % 2 else slice(0, 256)
        return dot3(field_high[:, cols], field_low[:, cols], lat[k, 0, used, :], lat[k, 1, used, :])

    ahead = lattice(0)
    for k in range(4):
        found = ahead
        if k < 3:
            ahead = lattice(k + 1)
        turn_re = twiddle[0:1, k * 256 : k * 256 + 256]
        turn_im = twiddle[1:2, k * 256 : k * 256 + 256]
        real = found[:, 0:256] * turn_re - found[:, 256:512] * turn_im
        imag = found[:, 0:256] * turn_im + found[:, 256:512] * turn_re
        flat = out.at[k].reshape(DEVICES * 8, 128)
        for half in range(2):
            sums = []
            for parity in range(2):
                rows = slice(parity * 256 + half * 128, parity * 256 + half * 128 + 128)
                high, low = split(jnp.concatenate([real[rows], imag[rows]], axis=0))
                at = parity * 2 + half
                sums.append(dot3(dep[0, at], dep[1, at], high, low))
            for b in range(2):
                both = sums[0] + sums[1] if b == 0 else sums[0] - sums[1]
                for ri in range(2):
                    for h in range(2):
                        at = half * 128 * 8 + (b * 2 + ri) * 2 + h
                        flat[pl.ds(at, 128, stride=8), :] = both[
                            ri * 128 : ri * 128 + 128, h * 128 : h * 128 + 128
                        ]
        leave.append(
            pltpu.make_async_copy(out.at[k], out_any.at[:, k * 8 : k * 8 + 8, :], sems.at[6 + k])
        )
        leave[k].start()
    for copy in leave:
        copy.wait()


def middle(got, twiddle):
    lat = jnp.asarray(np.stack(lattice_tables(), axis=1))
    dep = jnp.asarray(np.stack(depth_tables()))
    hbm = pl.BlockSpec(memory_space=pltpu.HBM)
    return pl.pallas_call(
        middle_kernel,
        out_shape=jax.ShapeDtypeStruct((DEVICES, 32, 128), F32),
        in_specs=[
            pl.BlockSpec(memory_space=pl.ANY),
            pl.BlockSpec(memory_space=pltpu.VMEM),
            hbm,
            hbm,
        ],
        out_specs=hbm,
        scratch_shapes=[
            pltpu.VMEM((DEVICES * CHUNK, 128), F32),
            pltpu.VMEM(lat.shape, BF16),
            pltpu.VMEM(dep.shape, BF16),
            pltpu.VMEM((NZ, SITES), BF16),
            pltpu.VMEM((NZ, SITES), BF16),
            pltpu.VMEM((2 * SLOTS * BRICK, 128), F32),
            pltpu.VMEM((LAYERS, DEVICES, 128), F32),
            pltpu.VMEM((4, DEVICES, 8, 128), F32),
            pltpu.SemaphoreType.DMA((10,)),
        ],
        compiler_params=pltpu.CompilerParams(vmem_limit_bytes=50 << 20),
        name="middle",
    )(got, twiddle, lat, dep)


def final_kernel(
    pieces_any, lap_z, lap_x, lap_y, cell_high, cell_low, out_re, out_im, pieces, held, sems
):
    block = lax.broadcasted_iota(jnp.int32, (8, 128), 1) // 32
    scale = -1.0 / math.sqrt(PLANE * PLANE * NZ)
    outs = (out_re, out_im)
    fetches = [
        pltpu.make_async_copy(pieces_any.at[:, k * 8 : k * 8 + 8, :], pieces.at[k], sems.at[k])
        for k in range(4)
    ]
    for fetch in fetches:
        fetch.start()
    for k in range(4):
        if k < 2:
            for fetch in fetches[:1] if k == 0 else fetches[1:]:
                fetch.wait()
        flat = pieces.at[k].reshape(DEVICES * 8, 128)
        for b in range(2):
            sides = []
            for side in range(2):
                parts = []
                for ri in range(2):
                    at = side * 128 * 8 + (b * 2 + ri) * 2
                    parts.append([flat[pl.ds(at + h, 128, stride=8), :] for h in range(2)])
                sides.append(jnp.concatenate([jnp.concatenate(p, axis=1) for p in parts], axis=0))
            folded = [split(sides[0] + sides[1]), split(sides[0] - sides[1])]
            results = [
                dot3(cell_high[odd, 0:128, :], cell_low[odd, 0:128, :], *folded[odd])
                for odd in range(2)
            ]
            along_z = lap_z[b]
            for h in range(2):
                along_x = [lap_x[k + 16 * h + 4 * r] + (along_z + SCREEN) for r in range(4)]
                for t in range(4):
                    tiles = []
                    for ri in range(2):
                        at = ri * 64 + t * 16
                        row = [
                            results[j % 2][
                                at + j // 2 * 8 : at + j // 2 * 8 + 8, h * 128 : h * 128 + 128
                            ]
                            for j in range(4)
                        ]
                        tiles.append(transpose_blocks(row, block))
                    for r in range(4):
                        kx = k + 16 * h + 4 * r
                        factor = scale / (along_x[r] + lap_y[t])
                        for ri in range(2):
                            held[ri, pl.ds(kx * 8 + t * 2 + b, 8, stride=PITCH), :] = (
                                tiles[ri][r] * factor
                            )
            if k > 0:
                continue
            lasts = [
                dot3(
                    cell_high[odd, 128:160, :], cell_low[odd, 128:160, :], folded[odd][0][:, :128], folded[odd][1][:, :128]
                )
                for odd in range(2)
            ]
            for ri in range(2):
                line = jnp.zeros((8, 128), F32)
                for j in range(4):
                    at = ri * 16 + j // 2 * 8
                    part = lasts[j % 2][at : at + 8, :]
                    moved = part if j == 0 else pltpu.roll(part, 32 * j, 1)
                    line = jnp.where(block == j, moved, line)
                for t in range(4):
                    factor = scale / (along_z + 4.0 + lap_y[t, 0:1] + SCREEN)
                    at = 8 * PITCH + t * 2 + b
                    held[ri, at : at + 1, :] = line[t : t + 1] * factor

    leave = []
    for ri in range(2):
        for k1x in range(9):
            count = 256 if k1x < 8 else 8
            kept = held.at[ri, pl.ds(k1x * PITCH, count), :]
            leave.append(
                pltpu.make_async_copy(kept, outs[ri].at[pl.ds(k1x * 256, count), :], sems.at[4 + ri * 9 + k1x])
            )
            leave[-1].start()
    for copy in leave:
        copy.wait()


def transpose_blocks(row, block):
    low, even = block < 2, block % 2 == 0
    first = [jnp.where(low, row[j], pltpu.roll(row[j + 2], 64, 1)) for j in range(2)]
    last = [jnp.where(low, pltpu.roll(row[j], 64, 1), row[j + 2]) for j in range(2)]
    tiles = []
    for a, b in (first, last):
        tiles.append(jnp.where(even, a, pltpu.roll(b, 32, 1)))
        tiles.append(jnp.where(even, pltpu.roll(a, 96, 1), b))
    return tiles


def final(pieces, lap_z):
    lap_x, lap_y = lap_tables()
    tables = [jnp.asarray(t) for t in (lap_x, lap_y, *cell_tables())]
    shape = jax.ShapeDtypeStruct((KX * 8, 128), F32)
    vmem = pl.BlockSpec(memory_space=pltpu.VMEM)
    outs = pl.pallas_call(
        final_kernel,
        out_shape=(shape, shape),
        in_specs=[
            pl.BlockSpec(memory_space=pl.ANY),
            pl.BlockSpec(memory_space=pltpu.SMEM),
            *[vmem] * 4,
        ],
        out_specs=(pl.BlockSpec(memory_space=pltpu.HBM), pl.BlockSpec(memory_space=pltpu.HBM)),
        scratch_shapes=[
            pltpu.VMEM((4, DEVICES, 8, 128), F32),
            pltpu.VMEM((2, 8 * PITCH + 8, 128), F32),
            pltpu.SemaphoreType.DMA((22,)),
        ],
        compiler_params=pltpu.CompilerParams(vmem_limit_bytes=24 << 20),
        name="final",
    )(pieces, lap_z, *tables)
    return tuple(
        o.reshape(KX, 4, 2, 128).transpose(2, 0, 1, 3).reshape(2, KX, PLANE) for o in outs
    )


def twiddle_of(device):
    yy = device // BRICK
    xx = device % BRICK
    column = jnp.arange(SITES, dtype=jnp.int32)
    kx = column // 256 + 4 * (column % 256 // BLOCKS)
    turn = (kx * xx + (column % BLOCKS) * yy) % PLANE
    angle = (2.0 * math.pi / PLANE) * turn.astype(F32)
    return jnp.stack([jnp.cos(angle), -jnp.sin(angle)])


def lap_z_of(device):
    kz = reverse_bits(2 * device + jnp.arange(2, dtype=jnp.int32), 9)
    return 4.0 * jnp.sin(math.pi * kz.astype(F32) / NZ) ** 2


def on_device(brick_data, brick_xy, brick_live):
    device = lax.axis_index("zg") * 32 + lax.axis_index("zl")
    sent = send(brick_data.reshape(SLOTS * BRICK, 256), brick_xy, brick_live.T)
    got = lax.all_to_all(sent.reshape(DEVICES, 1, CHUNK * 128), AXES, 0, 0, tiled=True)
    rows = middle(got.reshape(DEVICES * CHUNK, 128), twiddle_of(device))
    pieces = lax.all_to_all(rows, AXES, 0, 0, tiled=True)
    return final(pieces, lap_z_of(device))


def solution(mesh):
    in_specs = (P(AXES, None, None), P(None, AXES), P(None, AXES))
    out_specs = (P(AXES, None, None), P(AXES, None, None))
    return jax.shard_map(
        on_device, mesh=mesh, in_specs=in_specs, out_specs=out_specs, check_vma=False
    )
```

```python
import math

import jax
import jax.numpy as jnp
import numpy as np
from jax import lax
from jax.experimental import pallas as pl
from jax.experimental.pallas import tpu as pltpu
from jax.sharding import PartitionSpec as P

AXES = ("zg", "zl")
NZ = 512
PLANE = 512
BRICK = 16
BLOCKS = 32
LAYERS = 4
CAP = 16
GROUPS = 8
DEVICES = 256
KX = 257
SLOTS = LAYERS * CAP
SITES = BLOCKS * BLOCKS
SCREEN = 0.25
PITCH = 264
TOGETHER = 4
CHUNK = 9
BF16 = jnp.bfloat16
F32 = jnp.float32


def reverse_bits(values, digits):
    result = values * 0
    for digit in range(digits):
        result = result | ((values >> digit) & 1) << (digits - 1 - digit)
    return result


def halves_np(table):
    high = table.astype(np.float32).astype(jnp.bfloat16)
    low = (table - high.astype(np.float64)).astype(np.float32).astype(jnp.bfloat16)
    return high, low


def lattice_tables():
    inner, by = np.divmod(np.arange(256), BLOCKS)
    k_high, ky = np.divmod(np.arange(256), BLOCKS)
    tables = []
    for k_low in range(4):
        turn = inner[:, None] * (k_low + 4 * k_high)[None, :] + by[:, None] * ky[None, :]
        angle = 2.0 * np.pi * (turn % BLOCKS) / BLOCKS
        real, imag = np.cos(angle), -np.sin(angle)
        if k_low == 1:
            below = [imag, -real]
        elif k_low == 3:
            below = [-imag, real]
        else:
            below = [0.0 * real, 0.0 * real]
        tables.append(np.block([[real, imag], below]))
    return halves_np(np.stack(tables))


def depth_tables():
    device = np.arange(DEVICES)
    kz_all = reverse_bits(2 * device, 9)
    q, g, zh = np.meshgrid(np.arange(LAYERS), np.arange(4), np.arange(8), indexing="ij")
    tables = []
    for parity in range(2):
        for half in range(2):
            kz = kz_all[half * 128 : half * 128 + 128]
            z = (g * 64 + q * 16 + 2 * zh + parity).reshape(-1)
            angle = 2.0 * np.pi * (kz[:, None] * z[None, :] % NZ) / NZ
            cos, sin = np.cos(angle), np.sin(angle)
            tables.append(np.block([[cos, sin], [-sin, cos]]))
    return halves_np(np.stack(tables))


def cell_tables():
    yy, xx = np.divmod(np.arange(128), BRICK)

    def block(k1y, k1x):
        angle = 2.0 * np.pi * ((k1y[:, None] * yy + k1x[:, None] * xx) % BRICK) / BRICK
        cos, sin = np.cos(angle), np.sin(angle)
        return np.block([[cos, sin], [-sin, cos]])

    tables = []
    for odd in range(2):
        t, j, k1x = (a.reshape(-1) for a in np.meshgrid(np.arange(4), np.arange(2), np.arange(8), indexing="ij"))
        main = block(4 * t + 2 * j + odd, k1x)
        j, t = (a.reshape(-1) for a in np.meshgrid(np.arange(2), np.arange(8), indexing="ij"))
        last = block(4 * (t % 4) + 2 * j + odd, np.full(16, 8))
        tables.append(np.concatenate([main, last], axis=0))
    return halves_np(np.stack(tables))


def lap_tables():
    along_x = 4.0 * np.sin(np.pi * np.arange(288) / PLANE) ** 2
    along_y = 4.0 * np.sin(np.pi * np.arange(PLANE) / PLANE) ** 2
    rows = along_x[:256].reshape(8, 32).T
    lap_x = np.broadcast_to(rows[:, :, None], (32, 8, 128)).astype(np.float32)
    lap_y = np.broadcast_to(along_y.reshape(4, 1, 128), (4, 8, 128)).astype(np.float32)
    return lap_x, lap_y


def split(values):
    high = values.astype(BF16)
    return high, (values - high.astype(F32)).astype(BF16)


def dot(a, b):
    return jnp.dot(a, b, preferred_element_type=F32)


def dot3(a_high, a_low, b_high, b_low):
    return dot(a_high, b_high) + dot(a_high, b_low) + dot(a_low, b_high)


def send_kernel(bricks, xy, live, out):
    for i in range(8):
        out[pl.ds(i, 128, stride=CHUNK), :] = bricks[i * 128 : i * 128 + 128, :].T
    slot = lax.broadcasted_iota(jnp.int32, (1, SLOTS), 1)
    count = jnp.zeros((1, SLOTS), jnp.int32)
    for q in range(LAYERS):
        count = jnp.where(slot // CAP == q, live[0, q], count)
    place = jnp.where(slot % CAP < count, xy[0:1, :] * BLOCKS + xy[1:2, :], -1)
    place = jnp.concatenate([place, jnp.full((1, 128 - SLOTS), -1, jnp.int32)], axis=1)
    out[pl.ds(8, 128, stride=CHUNK), :] = jnp.broadcast_to(place.astype(F32), (128, 128))


def send(bricks, xy, live):
    return pl.pallas_call(
        send_kernel,
        grid=(2,),
        out_shape=jax.ShapeDtypeStruct((DEVICES * CHUNK, 128), F32),
        in_specs=[
            pl.BlockSpec((SLOTS * BRICK, 128), lambda h: (0, h)),
            pl.BlockSpec(memory_space=pltpu.VMEM),
            pl.BlockSpec(memory_space=pltpu.SMEM),
        ],
        out_specs=pl.BlockSpec((128 * CHUNK, 128), lambda h: (h, 0)),
        compiler_params=pltpu.CompilerParams(vmem_limit_bytes=56 << 20),
        name="send",
    )(bricks, xy, live)


def read_cells(got, cells, places):
    for i in range(8):
        block = got[pl.ds(i, DEVICES, stride=CHUNK), :].T
        for h in range(2):
            at = h * 1024 + i * 128
            cells[at : at + 128, :] = block[:, h * 128 : h * 128 + 128]
    codes = got[pl.ds(8, DEVICES, stride=CHUNK), :]
    for q in range(LAYERS):
        places[q] = codes if q == 0 else pltpu.roll(codes, 128 - q * CAP, 1)


def spread_cells(cells, q, c, h, lane_group):
    tops, lows = [], []
    for parity in range(2):
        row = cells[pl.ds(h * 1024 + q * 256 + c * 16 + parity, 8, stride=2), :]
        tops.append(row.astype(BF16).astype(F32))
        lows.append(row - tops[-1])
    spread = [jnp.where(lane_group == g, piece, 0.0) for piece in tops + lows for g in range(4)]
    return jnp.concatenate(spread, axis=0).astype(BF16)


def place_layers(cells, places, field_high, field_low):
    lane_group = lax.broadcasted_iota(jnp.int32, (8, 128), 1) // 32
    site = lax.broadcasted_iota(jnp.int32, (128, SITES), 1).astype(F32)

    def place_layer(q, _):
        layers = []
        for h in range(2):
            where = places[q, h * 128 : h * 128 + 128, :]
            total = None
            for first in range(0, CAP, TOGETHER):
                slots = range(first, first + TOGETHER)
                spread = [spread_cells(cells, q, c, h, lane_group) for c in slots]
                chosen = [jnp.where(where[:, c : c + 1] == site, 1.0, 0.0).astype(BF16) for c in slots]
                part = dot(jnp.concatenate(spread, axis=1), jnp.concatenate(chosen, axis=0))
                total = part if total is None else total + part
            layers.append(total[:64] + total[64:])
        for half, layer in enumerate((layers[0] + layers[1], layers[0] - layers[1])):
            x = [layer[:, k * 256 : k * 256 + 256] for k in range(4)]
            even, odd = x[0] + x[2], x[1] + x[3]
            high, low = split(
                jnp.concatenate([even + odd, even - odd, x[0] - x[2], x[1] - x[3]], axis=1)
            )
            for parity in range(2):
                at = pl.multiple_of(parity * 256 + half * 128 + q * 32, 32)
                field_high[pl.ds(at, 32), :] = high[parity * 32 : parity * 32 + 32]
                field_low[pl.ds(at, 32), :] = low[parity * 32 : parity * 32 + 32]
        return 0

    lax.fori_loop(0, LAYERS, place_layer, 0, unroll=True)


def middle_kernel(
    got_any, twiddle, lat_any, dep_any, out_any,
    got, lat, dep, field_high, field_low, cells, places, out, sems,
):
    fetch_got = pltpu.make_async_copy(got_any, got, sems.at[0])
    fetch_got.start()
    fetch_dep = pltpu.make_async_copy(dep_any, dep, sems.at[1])
    fetch_dep.start()
    fetch_lat = [pltpu.make_async_copy(lat_any.at[k], lat.at[k], sems.at[2 + k]) for k in range(4)]
    for fetch in fetch_lat:
        fetch.start()
    fetch_got.wait()
    read_cells(got, cells, places)
    place_layers(cells, places, field_high, field_low)
    for fetch in (fetch_dep, *fetch_lat):
        fetch.wait()
    leave = []

    def lattice(k):
        cols = slice(512, 1024) if k % 2 else slice(k * 128, k * 128 + 256)
        used = slice(0, 512) if k % 2 else slice(0, 256)
        return dot3(field_high[:, cols], field_low[:, cols], lat[k, 0, used, :], lat[k, 1, used, :])

    ahead = lattice(0)
    for k in range(4):
        found = ahead
        if k < 3:
            ahead = lattice(k + 1)
        turn_re = twiddle[0:1, k * 256 : k * 256 + 256]
        turn_im = twiddle[1:2, k * 256 : k * 256 + 256]
        real = found[:, 0:256] * turn_re - found[:, 256:512] * turn_im
        imag = found[:, 0:256] * turn_im + found[:, 256:512] * turn_re
        flat = out.at[k].reshape(DEVICES * 8, 128)
        for half in range(2):
            sums = []
            for parity in range(2):
                rows = slice(parity * 256 + half * 128, parity * 256 + half * 128 + 128)
                high, low = split(jnp.concatenate([real[rows], imag[rows]], axis=0))
                at = parity * 2 + half
                sums.append(dot3(dep[0, at], dep[1, at], high, low))
            for b in range(2):
                both = sums[0] + sums[1] if b == 0 else sums[0] - sums[1]
                for ri in range(2):
                    for h in range(2):
                        at = half * 128 * 8 + (b * 2 + ri) * 2 + h
                        flat[pl.ds(at, 128, stride=8), :] = both[
                            ri * 128 : ri * 128 + 128, h * 128 : h * 128 + 128
                        ]
            rows = slice(half * 128, half * 128 + 128)
            leave.append(
                pltpu.make_async_copy(
                    out.at[k, rows], out_any.at[rows, k * 8 : k * 8 + 8, :], sems.at[6 + k * 2 + half]
                )
            )
            leave[-1].start()
    for copy in leave:
        copy.wait()


def middle(got, twiddle):
    lat = jnp.asarray(np.stack(lattice_tables(), axis=1))
    dep = jnp.asarray(np.stack(depth_tables()))
    hbm = pl.BlockSpec(memory_space=pltpu.HBM)
    return pl.pallas_call(
        middle_kernel,
        out_shape=jax.ShapeDtypeStruct((DEVICES, 32, 128), F32),
        in_specs=[
            pl.BlockSpec(memory_space=pl.ANY),
            pl.BlockSpec(memory_space=pltpu.VMEM),
            hbm,
            hbm,
        ],
        out_specs=hbm,
        scratch_shapes=[
            pltpu.VMEM((DEVICES * CHUNK, 128), F32),
            pltpu.VMEM(lat.shape, BF16),
            pltpu.VMEM(dep.shape, BF16),
            pltpu.VMEM((NZ, SITES), BF16),
            pltpu.VMEM((NZ, SITES), BF16),
            pltpu.VMEM((2 * SLOTS * BRICK, 128), F32),
            pltpu.VMEM((LAYERS, DEVICES, 128), F32),
            pltpu.VMEM((4, DEVICES, 8, 128), F32),
            pltpu.SemaphoreType.DMA((14,)),
        ],
        compiler_params=pltpu.CompilerParams(vmem_limit_bytes=50 << 20),
        name="middle",
    )(got, twiddle, lat, dep)


def final_kernel(
    pieces_any, lap_z, lap_x, lap_y, cell_high, cell_low, out_re, out_im, pieces, held, sems
):
    block = lax.broadcasted_iota(jnp.int32, (8, 128), 1) // 32
    scale = -1.0 / math.sqrt(PLANE * PLANE * NZ)
    outs = (out_re, out_im)
    fetches = [
        pltpu.make_async_copy(pieces_any.at[:, k * 8 : k * 8 + 8, :], pieces.at[k], sems.at[k])
        for k in range(4)
    ]
    for fetch in fetches:
        fetch.start()
    for k in range(4):
        if k < 2:
            for fetch in fetches[:1] if k == 0 else fetches[1:]:
                fetch.wait()
        flat = pieces.at[k].reshape(DEVICES * 8, 128)
        for b in range(2):
            sides = []
            for side in range(2):
                parts = []
                for ri in range(2):
                    at = side * 128 * 8 + (b * 2 + ri) * 2
                    parts.append([flat[pl.ds(at + h, 128, stride=8), :] for h in range(2)])
                sides.append(jnp.concatenate([jnp.concatenate(p, axis=1) for p in parts], axis=0))
            folded = [split(sides[0] + sides[1]), split(sides[0] - sides[1])]
            results = [
                dot3(cell_high[odd, 0:128, :], cell_low[odd, 0:128, :], *folded[odd])
                for odd in range(2)
            ]
            along_z = lap_z[b]
            for h in range(2):
                along_x = [lap_x[k + 16 * h + 4 * r] + (along_z + SCREEN) for r in range(4)]
                for t in range(4):
                    tiles = []
                    for ri in range(2):
                        at = ri * 64 + t * 16
                        row = [
                            results[j % 2][
                                at + j // 2 * 8 : at + j // 2 * 8 + 8, h * 128 : h * 128 + 128
                            ]
                            for j in range(4)
                        ]
                        tiles.append(transpose_blocks(row, block))
                    for r in range(4):
                        kx = k + 16 * h + 4 * r
                        factor = scale / (along_x[r] + lap_y[t])
                        for ri in range(2):
                            held[ri, pl.ds(kx * 8 + t * 2 + b, 8, stride=PITCH), :] = (
                                tiles[ri][r] * factor
                            )
            if k > 0:
                continue
            lasts = [
                dot3(
                    cell_high[odd, 128:160, :], cell_low[odd, 128:160, :], folded[odd][0][:, :128], folded[odd][1][:, :128]
                )
                for odd in range(2)
            ]
            for ri in range(2):
                line = jnp.zeros((8, 128), F32)
                for j in range(4):
                    at = ri * 16 + j // 2 * 8
                    part = lasts[j % 2][at : at + 8, :]
                    moved = part if j == 0 else pltpu.roll(part, 32 * j, 1)
                    line = jnp.where(block == j, moved, line)
                for t in range(4):
                    factor = scale / (along_z + 4.0 + lap_y[t, 0:1] + SCREEN)
                    at = 8 * PITCH + t * 2 + b
                    held[ri, at : at + 1, :] = line[t : t + 1] * factor

    leave = []
    for ri in range(2):
        for k1x in range(9):
            count = 256 if k1x < 8 else 8
            kept = held.at[ri, pl.ds(k1x * PITCH, count), :]
            leave.append(
                pltpu.make_async_copy(kept, outs[ri].at[pl.ds(k1x * 256, count), :], sems.at[4 + ri * 9 + k1x])
            )
            leave[-1].start()
    for copy in leave:
        copy.wait()


def transpose_blocks(row, block):
    low, even = block < 2, block % 2 == 0
    first = [jnp.where(low, row[j], pltpu.roll(row[j + 2], 64, 1)) for j in range(2)]
    last = [jnp.where(low, pltpu.roll(row[j], 64, 1), row[j + 2]) for j in range(2)]
    tiles = []
    for a, b in (first, last):
        tiles.append(jnp.where(even, a, pltpu.roll(b, 32, 1)))
        tiles.append(jnp.where(even, pltpu.roll(a, 96, 1), b))
    return tiles


def final(pieces, lap_z):
    lap_x, lap_y = lap_tables()
    tables = [jnp.asarray(t) for t in (lap_x, lap_y, *cell_tables())]
    shape = jax.ShapeDtypeStruct((KX * 8, 128), F32)
    vmem = pl.BlockSpec(memory_space=pltpu.VMEM)
    outs = pl.pallas_call(
        final_kernel,
        out_shape=(shape, shape),
        in_specs=[
            pl.BlockSpec(memory_space=pl.ANY),
            pl.BlockSpec(memory_space=pltpu.SMEM),
            *[vmem] * 4,
        ],
        out_specs=(pl.BlockSpec(memory_space=pltpu.HBM), pl.BlockSpec(memory_space=pltpu.HBM)),
        scratch_shapes=[
            pltpu.VMEM((4, DEVICES, 8, 128), F32),
            pltpu.VMEM((2, 8 * PITCH + 8, 128), F32),
            pltpu.SemaphoreType.DMA((22,)),
        ],
        compiler_params=pltpu.CompilerParams(vmem_limit_bytes=24 << 20),
        name="final",
    )(pieces, lap_z, *tables)
    return tuple(
        o.reshape(KX, 4, 2, 128).transpose(2, 0, 1, 3).reshape(2, KX, PLANE) for o in outs
    )


def twiddle_of(device):
    yy = device // BRICK
    xx = device % BRICK
    column = jnp.arange(SITES, dtype=jnp.int32)
    kx = column // 256 + 4 * (column % 256 // BLOCKS)
    turn = (kx * xx + (column % BLOCKS) * yy) % PLANE
    angle = (2.0 * math.pi / PLANE) * turn.astype(F32)
    return jnp.stack([jnp.cos(angle), -jnp.sin(angle)])


def lap_z_of(device):
    kz = reverse_bits(2 * device + jnp.arange(2, dtype=jnp.int32), 9)
    return 4.0 * jnp.sin(math.pi * kz.astype(F32) / NZ) ** 2


def on_device(brick_data, brick_xy, brick_live):
    device = lax.axis_index("zg") * 32 + lax.axis_index("zl")
    sent = send(brick_data.reshape(SLOTS * BRICK, 256), brick_xy, brick_live.T)
    got = lax.all_to_all(sent.reshape(DEVICES, 1, CHUNK * 128), AXES, 0, 0, tiled=True)
    rows = middle(got.reshape(DEVICES * CHUNK, 128), twiddle_of(device))
    pieces = lax.all_to_all(rows, AXES, 0, 0, tiled=True)
    return final(pieces, lap_z_of(device))


def solution(mesh):
    in_specs = (P(AXES, None, None), P(None, AXES), P(None, AXES))
    out_specs = (P(AXES, None, None), P(AXES, None, None))
    return jax.shard_map(
        on_device, mesh=mesh, in_specs=in_specs, out_specs=out_specs, check_vma=False
    )
```
